128 devices in a mesh: shard: 32 (over z, y, core), tensor: 4 (over x).
Axes of the slice: x: 4, y: 4, z: 4, core: 2. Of those that a mesh axis runs over, the one named last changes fastest.
Arguments:
- attn_weight: float32 [4, 2048, 2048], P(None, 'shard', 'tensor'), may hold values from -62 to 62
- ffin_weight: float32 [2, 2048, 5120], P(None, 'shard', 'tensor'), may hold values from -62 to 62
- ffout_weight: float32 [1, 5120, 2048], P(None, 'shard', 'tensor'), may hold values from -62 to 62
- attn_grad: float32 [4, 2048, 2048], P(None, 'shard', 'tensor'), may hold values from -62 to 62
- ffin_grad: float32 [2, 2048, 5120], P(None, 'shard', 'tensor'), may hold values from -62 to 62
- ffout_grad: float32 [1, 5120, 2048], P(None, 'shard', 'tensor'), may hold values from -62 to 62
- attn_first: float32 [4, 2048, 2048], P(None, ('shard', 'tensor')), may hold values from -62 to 62
- ffin_first: float32 [2, 5120, 2048], P(None, ('shard', 'tensor')), may hold values from -62 to 62
- ffout_first: float32 [1, 2048, 5120], P(None, ('shard', 'tensor')), may hold values from -62 to 62
- attn_second: float32 [4, 2048, 2048], P(None, ('shard', 'tensor')), may hold values from 0.01 to 1
- ffin_second: float32 [2, 5120, 2048], P(None, ('shard', 'tensor')), may hold values from 0.01 to 1
- ffout_second: float32 [1, 2048, 5120], P(None, ('shard', 'tensor')), may hold values from 0.01 to 1
Outputs:
- attn_new: float32 [4, 2048, 2048], P(None, 'shard', 'tensor')
- ffin_new: float32 [2, 2048, 5120], P(None, 'shard', 'tensor')
- ffout_new: float32 [1, 5120, 2048], P(None, 'shard', 'tensor')
- attn_first_new: float32 [4, 2048, 2048], P(None, ('shard', 'tensor'))
- ffin_first_new: float32 [2, 5120, 2048], P(None, ('shard', 'tensor'))
- ffout_first_new: float32 [1, 2048, 5120], P(None, ('shard', 'tensor'))
- attn_second_new: float32 [4, 2048, 2048], P(None, ('shard', 'tensor'))
- ffin_second_new: float32 [2, 5120, 2048], P(None, ('shard', 'tensor'))
- ffout_second_new: float32 [1, 2048, 5120], P(None, ('shard', 'tensor'))
- trust_ratio: float32 [7], replicated
The draws below stay inside these ranges and needn't reach their ends.
All inputs are finite; a program needn't handle non-finite values.
Results may differ from the reference program's by a relative error of at most 0.00002.
Values sent between devices are 32-bit elements; how exact they have to be, the bound alone decides.
No kernel may reach another device: no remote copies, remote signals or barrier semaphores. Data moves between devices by JAX's collectives and lax.ppermute only.
A program may use at most 64 MiB of HBM per device.

```python
import math
import jax
import jax.numpy as jnp
from jax import lax

D = 2048
FF = 5120


def rough_field(key, shape, row_dim, col_dim):
    key_base, key_rows, key_cols = jax.random.split(key, 3)
    base = jnp.clip(jax.random.normal(key_base, shape, jnp.float32), -6.0, 6.0)
    row_count = shape[row_dim]
    col_count = shape[col_dim]
    row_scale = 10.0 ** (0.5 * jax.random.uniform(key_rows, (row_count,), jnp.float32) - 0.25)
    row_scale = row_scale * (1.0 + 0.8 * jnp.arange(row_count, dtype=jnp.float32) / row_count)
    col_scale = 10.0 ** (0.5 * jax.random.uniform(key_cols, (col_count,), jnp.float32) - 0.25)
    col_scale = col_scale * (1.0 + 0.8 * jnp.arange(col_count, dtype=jnp.float32) / col_count)
    row_shape = [1] * len(shape)
    row_shape[row_dim] = row_count
    col_shape = [1] * len(shape)
    col_shape[col_dim] = col_count
    return base * row_scale.reshape(row_shape) * col_scale.reshape(col_shape)


def draw_attn_weight(key, part):
    return rough_field(jax.random.fold_in(key, 11), (4, D, D), 1, 2)


def draw_ffin_weight(key, part):
    return rough_field(jax.random.fold_in(key, 12), (2, D, FF), 1, 2)


def draw_ffout_weight(key, part):
    return rough_field(jax.random.fold_in(key, 13), (1, FF, D), 1, 2)


def draw_attn_grad(key, part):
    return rough_field(jax.random.fold_in(key, 21), (4, D, D), 1, 2)


def draw_ffin_grad(key, part):
    return rough_field(jax.random.fold_in(key, 22), (2, D, FF), 1, 2)


def draw_ffout_grad(key, part):
    return rough_field(jax.random.fold_in(key, 23), (1, FF, D), 1, 2)


def draw_attn_first(key, part):
    return rough_field(jax.random.fold_in(key, 31), (4, D, D), 2, 1)


def draw_ffin_first(key, part):
    return rough_field(jax.random.fold_in(key, 32), (2, FF, D), 2, 1)


def draw_ffout_first(key, part):
    return rough_field(jax.random.fold_in(key, 33), (1, D, FF), 2, 1)


def block_levels(stream_key, dims, pieces, low, largest):
    def one(axis_at, parts):
        draws = jax.random.uniform(jax.random.fold_in(jax.random.fold_in(stream_key, 6), axis_at), (parts,), jnp.float32, low / len(pieces), largest / len(pieces))
        return jnp.repeat(jnp.exp(draws), dims[axis_at] // parts).reshape((-1,) + (1,) * (len(dims) - axis_at - 1))

    gain = one(*pieces[0])
    for cut in pieces[1:]:
        gain = gain * one(*cut)
    return gain


def setup_inputs(seed: int = 0) -> dict:
    streams_of = jax.random.split(jax.random.key(seed), 13)
    attn_weight = draw_attn_weight(jax.random.fold_in(streams_of[12], 71), 0)
    ffin_weight = draw_ffin_weight(jax.random.fold_in(streams_of[12], 71), 0)
    ffout_weight = draw_ffout_weight(jax.random.fold_in(streams_of[12], 71), 0)
    attn_grad = draw_attn_grad(jax.random.fold_in(streams_of[12], 71), 0)
    ffin_grad = draw_ffin_grad(jax.random.fold_in(streams_of[12], 71), 0)
    ffout_grad = draw_ffout_grad(jax.random.fold_in(streams_of[12], 71), 0)
    attn_first = draw_attn_first(jax.random.fold_in(streams_of[12], 71), 0)
    ffin_first = draw_ffin_first(jax.random.fold_in(streams_of[12], 71), 0)
    ffout_first = draw_ffout_first(jax.random.fold_in(streams_of[12], 71), 0)
    attn_second = jnp.clip(jnp.exp(math.log(1.0) - 4.6051702 * jax.random.uniform(streams_of[9], (4, D, D), jnp.float32) ** block_levels(streams_of[9], (4, D, D), ((1, 128),), -0.2, 0.2)), 0.01, 1.0)
    ffin_second = jnp.clip(jnp.exp(math.log(1.0) - 4.6051702 * jax.random.uniform(streams_of[10], (2, FF, D), jnp.float32) ** block_levels(streams_of[10], (2, FF, D), ((1, 128),), -0.2, 0.2)), 0.01, 1.0)
    ffout_second = jnp.clip(jnp.exp(math.log(1.0) - 4.6051702 * jax.random.uniform(streams_of[11], (1, D, FF), jnp.float32) ** block_levels(streams_of[11], (1, D, FF), ((1, 128),), -0.2, 0.2)), 0.01, 1.0)
    return {"attn_weight": attn_weight, "ffin_weight": ffin_weight, "ffout_weight": ffout_weight, "attn_grad": attn_grad, "ffin_grad": ffin_grad, "ffout_grad": ffout_grad, "attn_first": attn_first, "ffin_first": ffin_first, "ffout_first": ffout_first, "attn_second": attn_second, "ffin_second": ffin_second, "ffout_second": ffout_second}


beta_one = 0.9
beta_two = 0.999
step_number = 10.0
correct_one = 1.0 - beta_one ** step_number
correct_two = 1.0 - beta_two ** step_number
learn_rate = 0.02
decay_rate = 0.1
epsilon = 1e-06

def moment_step(gradient_t, first_moment, second):
    first_new = beta_one * first_moment + (1.0 - beta_one) * gradient_t
    second_new = beta_two * second + (1.0 - beta_two) * gradient_t * gradient_t
    ratio_value = first_new / correct_one / (jnp.sqrt(second_new / correct_two) + epsilon)
    return (first_new, second_new, ratio_value)

def reference(attn_weight, ffin_weight, ffout_weight, attn_grad, ffin_grad, ffout_grad, attn_first, ffin_first, ffout_first, attn_second, ffin_second, ffout_second):
    weights = (attn_weight, ffin_weight, ffout_weight)
    gradients = (attn_grad, ffin_grad, ffout_grad)
    firsts = (attn_first, ffin_first, ffout_first)
    seconds = (attn_second, ffin_second, ffout_second)
    results = [moment_step(jnp.swapaxes(gradients[position], 1, 2), firsts[position], seconds[position]) for position in range(3)]
    updates = [jnp.swapaxes(results[position][2], 1, 2) + decay_rate * weights[position] for position in range(3)]
    weight_sq = jnp.concatenate([lax.optimization_barrier(jnp.sum(matrix * matrix, axis=(1, 2))) for matrix in weights])
    update_sq = jnp.concatenate([lax.optimization_barrier(jnp.sum(member * member, axis=(1, 2))) for member in updates])
    trust_ratio = jnp.sqrt(weight_sq) / (jnp.sqrt(update_sq) + epsilon)
    scales = (trust_ratio[0:4], trust_ratio[4:6], trust_ratio[6:7])
    new_weights = [weights[position] - learn_rate * scales[position][:, None, None] * updates[position] for position in range(3)]
    return (new_weights[0], new_weights[1], new_weights[2], results[0][0], results[1][0], results[2][0], results[0][1], results[1][1], results[2][1], trust_ratio)
```

```python
import functools

import jax
import jax.numpy as jnp
from jax import lax
from jax.experimental import pallas as pl
from jax.experimental.pallas import tpu as pltpu
from jax.sharding import PartitionSpec as P

beta_one = 0.9
beta_two = 0.999
step_number = 10.0
correct_one = 1.0 - beta_one**step_number
correct_two = 1.0 - beta_two**step_number
learn_rate = 0.02
decay_rate = 0.1
epsilon = 1e-06

F32 = jnp.float32
SHARDS = 32
SPLIT = 4
QS = SHARDS // SPLIT
ROWS = 96


def lanes(shape):
    return lax.broadcasted_iota(jnp.int32, shape, len(shape) - 1)


def roll(x, shift):
    shift %= 128
    return pltpu.roll(x, shift, x.ndim - 1) if shift else x


def swap_halves(x0, x1):
    low = lanes(x0.shape) < 64
    return jnp.where(low, x0, roll(x1, 64)), jnp.where(low, roll(x0, 64), x1)


def pack_moments(attn, ffin, ffout, out, base):
    for half in range(2):
        cols = slice(half * 128, half * 128 + 128)
        for pair in range(2):
            x0, x1 = swap_halves(attn[2 * pair, :, cols], attn[2 * pair + 1, :, cols])
            rows = slice(base + 16 * pair, base + 16 * pair + 16)
            out[2 * half, rows, :] = x0
            out[2 * half + 1, rows, :] = x1
        x0, x1 = swap_halves(ffin[0, :, cols], ffin[1, :, cols])
        out[2 * half, base + 32 : base + 72, :] = x0
        out[2 * half + 1, base + 32 : base + 72, :] = x1
    lane = lanes((16, 128))
    for e in range(4):
        x = roll(ffout[0, :, e * 128 : e * 128 + 128], -32 * e)
        y = roll(ffout[0, :, e * 128 + 128 : e * 128 + 256], -32 * e)
        out[e, base + 72 : base + 88, :] = jnp.where(lane < 128 - 32 * e, x, y)
        last = jnp.where(lane[:8] < 64, roll(y[8:16], 32), 0.0)
        out[e, base + 88 : base + 96, :] = jnp.where(lane[:8] < 32, y[0:8], last)


def k0_body(am, fm, om, av, fv, ov, out):
    pack_moments(am, fm, om, out, 0)
    pack_moments(av, fv, ov, out, ROWS)


def moment_specs():
    return [
        pl.BlockSpec((4, 16, 256), lambda i, *_: (0, 0, i)),
        pl.BlockSpec((2, 40, 256), lambda i, *_: (0, 0, i)),
        pl.BlockSpec((1, 16, 640), lambda i, *_: (0, 0, i)),
    ]


def pack_mv(am, fm, om, av, fv, ov):
    return pl.pallas_call(
        k0_body,
        grid=(8,),
        in_specs=moment_specs() * 2,
        out_specs=pl.BlockSpec((4, 2 * ROWS, 128), lambda i: (i, 0, 0)),
        out_shape=jax.ShapeDtypeStruct((SHARDS, 2 * ROWS, 128), F32),
        name="pack_mv",
    )(am, fm, om, av, fv, ov)


def k1_body(me, attn, ffin, ffout, o0, o1, o2, o3, turned):
    outs = (o0, o1, o2, o3)
    lane = lanes((8, 128))
    for pair in range(2):
        both = jnp.concatenate([attn[2 * pair], attn[2 * pair + 1]], axis=0)
        turned[pair * 256 : pair * 256 + 256, :] = both.T
    turned[512:1152, :] = jnp.concatenate([ffin[0], ffin[1]], axis=0).T
    turned[1152:1408, :] = ffout[0, 0:128, :].T
    last = jnp.concatenate([ffout[0, 128:160, :], jnp.zeros((96, 256), F32)], axis=0)
    turned[1408:1664, :] = last.T
    for d in range(SPLIT):
        target = lax.rem(me[0] + d, SPLIT)
        for q in range(4):
            place = q * SPLIT + target
            at = pl.multiple_of(place * 16, 16)
            for pair in range(2):
                outs[d][q, 16 * pair : 16 * pair + 16, :] = turned[pl.ds(pair * 256 + at, 16), :]
            outs[d][q, 32:72, :] = turned[pl.ds(512 + pl.multiple_of(place * 40, 8), 40), :]
            outs[d][q, 72:88, :] = turned[pl.ds(1152 + at, 16), :]
            v0 = turned[pl.ds(1408 + at, 8), :]
            v1 = turned[pl.ds(1416 + at, 8), :]
            outs[d][q, 88:96, :] = jnp.where(lane < 32, v0, roll(v1, 32))


def weight_specs():
    return [
        pl.BlockSpec((4, 64, 256), lambda i, *_: (0, 0, i)),
        pl.BlockSpec((2, 64, 640), lambda i, *_: (0, 0, i)),
        pl.BlockSpec((1, 160, 256), lambda i, *_: (0, 0, i)),
    ]


def pack_home(me, attn, ffin, ffout, name):
    return pl.pallas_call(
        k1_body,
        grid_spec=pltpu.PrefetchScalarGridSpec(
            num_scalar_prefetch=1,
            grid=(2,),
            in_specs=weight_specs(),
            out_specs=[pl.BlockSpec((4, ROWS, 128), lambda i, *_: (i, 0, 0))] * 4,
            scratch_shapes=[pltpu.VMEM((1664, 128), F32)],
        ),
        out_shape=[jax.ShapeDtypeStruct((QS, ROWS, 128), F32)] * 4,
        name=name,
    )(me, attn, ffin, ffout)


GROUPS = ((0, 16), (16, 32), (32, 72), (72, 96))


def k3a_body(sel, mv, g, w, u, acc):
    @pl.when(pl.program_id(0) == 0)
    def _():
        acc[...] = jnp.zeros_like(acc)

    for n, (lo, hi) in enumerate(GROUPS):
        gt = g[:, lo:hi, :]
        first = beta_one * mv[:, lo:hi, :] + (1.0 - beta_one) * gt
        second = beta_two * mv[:, ROWS + lo : ROWS + hi, :] + (1.0 - beta_two) * gt * gt
        ratio = first / correct_one / (jnp.sqrt(second / correct_two) + epsilon)
        weight = w[:, lo:hi, :]
        update = ratio + decay_rate * weight
        u[:, lo:hi, :] = update
        acc[n] += jnp.sum((update * update).reshape(-1, 8, 128), axis=0)
        acc[4 + n] += jnp.sum((weight * weight).reshape(-1, 8, 128), axis=0)


def make_update(sel, mv, g, w):
    return pl.pallas_call(
        k3a_body,
        grid_spec=pltpu.PrefetchScalarGridSpec(
            num_scalar_prefetch=1,
            grid=(2,),
            in_specs=[
                pl.BlockSpec((4, 2 * ROWS, 128), lambda i, sel: (2 * sel[0] + i, 0, 0)),
                pl.BlockSpec((4, ROWS, 128), lambda i, sel: (i, 0, 0)),
                pl.BlockSpec((4, ROWS, 128), lambda i, sel: (i, 0, 0)),
            ],
            out_specs=[
                pl.BlockSpec((4, ROWS, 128), lambda i, sel: (i, 0, 0)),
                pl.BlockSpec((8, 8, 128), lambda i, sel: (0, 0, 0)),
            ],
        ),
        out_shape=[
            jax.ShapeDtypeStruct((QS, ROWS, 128), F32),
            jax.ShapeDtypeStruct((8, 8, 128), F32),
        ],
        name="make_update",
    )(sel, mv, g, w)


def kga_body(me, g0, g1, g2, g3, a0, a1, a2, a3, out):
    total = jnp.sum(a0[...] + a1[...] + a2[...] + a3[...], axis=1)
    fold = total + roll(total, 96)
    lane = lanes((1, 128))
    rows = []
    for matrix in range(7):
        parts = []
        for kind in range(2):
            group = kind * 4 + (3 if matrix == 6 else matrix // 2)
            row = fold[group : group + 1]
            if matrix == 6:
                row = row + roll(row, 64)
            elif matrix % 2:
                row = roll(row, 64)
            parts.append(row)
        rows.append(jnp.where(lane < 96, roll(parts[0], 64), roll(parts[1], 96)))
    rows.append(jnp.zeros((1, 128), F32))
    sums = jnp.concatenate(rows, axis=0)
    keep = lanes((QS, 8, 128)) < 64
    for d, g in enumerate((g0, g1, g2, g3)):
        source = lax.rem(me[0] + SPLIT - d, SPLIT)
        at = pl.ds(source * QS, QS)
        out[at, 0:88, :] = g[:, 0:88, :]
        out[at, 88:96, :] = jnp.where(keep, g[:, 88:96, :], sums[None])


def gather_grads(me, gs, accs):
    return pl.pallas_call(
        kga_body,
        grid_spec=pltpu.PrefetchScalarGridSpec(
            num_scalar_prefetch=1,
            grid=(1,),
            in_specs=[pl.BlockSpec((QS, ROWS, 128), lambda i, *_: (0, 0, 0))] * 4
            + [pl.BlockSpec((8, 8, 128), lambda i, *_: (0, 0, 0))] * 4,
            out_specs=pl.BlockSpec((SHARDS, ROWS, 128), lambda i, *_: (0, 0, 0)),
        ),
        out_shape=jax.ShapeDtypeStruct((SHARDS, ROWS, 128), F32),
        name="gather_grads",
    )(me, *gs, *accs)


def ks_body(x, out):
    out[...] = jnp.sum(x[...], axis=0)


def add_sums(x):
    return pl.pallas_call(
        ks_body,
        grid=(1,),
        in_specs=[pl.BlockSpec((SHARDS, 8, 128), lambda i: (0, ROWS // 8 - 1, 0))],
        out_specs=pl.BlockSpec((8, 128), lambda i: (0, 0)),
        out_shape=jax.ShapeDtypeStruct((8, 128), F32),
        name="add_sums",
    )(x)


def k2_body(g, am, fm, om, av, fv, ov, am2, fm2, om2, av2, fv2, ov2):
    def step(at, grad, first, second, first_new, second_new):
        first_new[at] = beta_one * first[at] + (1.0 - beta_one) * grad
        second_new[at] = beta_two * second[at] + (1.0 - beta_two) * grad * grad

    every = slice(None)
    for half in range(2):
        cols = slice(half * 128, half * 128 + 128)
        for pair in range(2):
            rows = slice(16 * pair, 16 * pair + 16)
            x = swap_halves(g[2 * half, rows, :], g[2 * half + 1, rows, :])
            for a in range(2):
                step((2 * pair + a, every, cols), x[a], am, av, am2, av2)
        x = swap_halves(g[2 * half, 32:72, :], g[2 * half + 1, 32:72, :])
        for a in range(2):
            step((a, every, cols), x[a], fm, fv, fm2, fv2)
    lane = lanes((16, 128))
    before = rest = None
    for b in range(5):
        block = None
        if b < 4:
            block = roll(g[b, 72:88, :], 32 * b)
        here = block
        if b > 0:
            here = rest if block is None else jnp.where(lane < 32 * b, rest, block)
            here = jnp.where(lane < 32 * (b - 1), before, here)
        step((0, every, slice(b * 128, b * 128 + 128)), here, om, ov, om2, ov2)
        if b < 4:
            before = block
            tile = g[b, 88:96, :]
            rest = jnp.concatenate([roll(tile, 32 * b), roll(tile, 32 * b - 32)], axis=0)


def new_moments(g, am, fm, om, av, fv, ov):
    return pl.pallas_call(
        k2_body,
        grid=(8,),
        in_specs=[pl.BlockSpec((4, ROWS, 128), lambda i: (i, 0, 0))] + moment_specs() * 2,
        out_specs=moment_specs() * 2,
        out_shape=[jax.ShapeDtypeStruct(x.shape, F32) for x in (am, fm, om, av, fv, ov)],
        name="new_moments",
    )(g, am, fm, om, av, fv, ov)


def k3b_body(me, s0, s1, s2, s3, u0, u1, u2, u3, attn, ffin, ffout, attn2, ffin2, ffout2, trust_out, turned):
    total = (s0[...] + s2[...]) + (s1[...] + s3[...])
    lane = lanes((8, 128))
    update_sq = jnp.sum(jnp.where((lane >= 64) & (lane < 96), total, 0.0), axis=1, keepdims=True)
    weight_sq = jnp.sum(jnp.where(lane >= 96, total, 0.0), axis=1, keepdims=True)
    trust = jnp.sqrt(weight_sq) / (jnp.sqrt(update_sq) + epsilon)
    trust_out[...] = jnp.broadcast_to(trust, (8, 128))
    scale = learn_rate * trust
    for d, u in enumerate((u0, u1, u2, u3)):
        source = lax.rem(me[0] + d, SPLIT)
        for q in range(4):
            place = q * SPLIT + source
            at = pl.multiple_of(place * 16, 16)
            for pair in range(2):
                turned[pl.ds(pair * 256 + at, 16), :] = u[q, 16 * pair : 16 * pair + 16, :]
            turned[pl.ds(512 + pl.multiple_of(place * 40, 8), 40), :] = u[q, 32:72, :]
            turned[pl.ds(1152 + at, 16), :] = u[q, 72:88, :]
            tile = u[q, 88:96, :]
            turned[pl.ds(1408 + at, 8), :] = tile
            turned[pl.ds(1416 + at, 8), :] = roll(tile, -32)
    for pair in range(2):
        back = turned[pair * 256 : pair * 256 + 256, :].T
        for a in range(2):
            n = 2 * pair + a
            attn2[n] = attn[n] - scale[n : n + 1] * back[64 * a : 64 * a + 64]
    back = turned[512:1152, :].T
    for a in range(2):
        ffin2[a] = ffin[a] - scale[4 + a : 5 + a] * back[64 * a : 64 * a + 64]
    ffout2[0, 0:128, :] = ffout[0, 0:128, :] - scale[6:7] * turned[1152:1408, :].T
    ffout2[0, 128:160, :] = ffout[0, 128:160, :] - scale[6:7] * turned[1408:1664, :].T[0:32]


def new_weights(me, sums, us, attn, ffin, ffout):
    return pl.pallas_call(
        k3b_body,
        grid_spec=pltpu.PrefetchScalarGridSpec(
            num_scalar_prefetch=1,
            grid=(2,),
            in_specs=[pl.BlockSpec((8, 128), lambda i, *_: (0, 0))] * 4
            + [pl.BlockSpec((4, ROWS, 128), lambda i, *_: (i, 0, 0))] * 4
            + weight_specs(),
            out_specs=weight_specs() + [pl.BlockSpec((8, 128), lambda i, *_: (0, 0))],
            scratch_shapes=[pltpu.VMEM((1664, 128), F32)],
        ),
        out_shape=[jax.ShapeDtypeStruct(x.shape, F32) for x in (attn, ffin, ffout)]
        + [jax.ShapeDtypeStruct((8, 128), F32)],
        name="new_weights",
    )(me, *sums, *us, attn, ffin, ffout)


def along(x, shift):
    shift %= SPLIT
    if shift == 0:
        return x
    return lax.ppermute(x, "tensor", [(i, (i + shift) % SPLIT) for i in range(SPLIT)])


def shards(aw, fw, ow, ag, fg, og, am, fm, om, av, fv, ov):
    t = lax.axis_index("tensor").astype(jnp.int32)
    me = t.reshape(1)
    mv = pack_mv(am, fm, om, av, fv, ov)
    mv_here = lax.all_to_all(mv, "shard", split_axis=0, concat_axis=0, tiled=True)
    g = pack_home(me, ag, fg, og, "pack_grads")
    g = [along(g[d], d) for d in range(SPLIT)]
    w = pack_home(me, aw, fw, ow, "pack_weights")
    w = [along(w[d], d) for d in range(SPLIT)]
    us, accs = [None] * SPLIT, [None] * SPLIT
    for d in (1, 3, 2, 0):
        sel = jnp.remainder(t + SPLIT - d, SPLIT).reshape(1)
        u, accs[d] = make_update(sel, mv_here, g[d], w[d])
        us[d] = along(u, -d)
    grads = gather_grads(me, g, accs)
    grads = lax.all_to_all(grads, "shard", split_axis=0, concat_axis=0, tiled=True)
    sums = add_sums(grads)
    sums = [along(sums, d) for d in range(SPLIT)]
    moments = new_moments(grads, am, fm, om, av, fv, ov)
    aw2, fw2, ow2, trust = new_weights(me, sums, us, aw, fw, ow)
    return (aw2, fw2, ow2, *moments, trust[:7, 0])


def solution(mesh):
    home = P(None, "shard", "tensor")
    flat = P(None, ("shard", "tensor"), None)
    in_specs = (home,) * 6 + (flat,) * 6
    out_specs = (home,) * 3 + (flat,) * 6 + (P(),)
    return jax.shard_map(shards, mesh=mesh, in_specs=in_specs, out_specs=out_specs, check_vma=False)
```

```python
import jax
import jax.numpy as jnp
from jax import lax
from jax.experimental import pallas as pl
from jax.experimental.pallas import tpu as pltpu
from jax.sharding import PartitionSpec as P

beta_one = 0.9
beta_two = 0.999
step_number = 10.0
correct_one = 1.0 - beta_one**step_number
correct_two = 1.0 - beta_two**step_number
learn_rate = 0.02
decay_rate = 0.1
epsilon = 1e-06

F32 = jnp.float32
SHARDS = 32
SPLIT = 4
QS = SHARDS // SPLIT
HEAD = 88
ROWS = 96


ANY = pl.BlockSpec(memory_space=pl.ANY)
VSPEC = pl.BlockSpec(memory_space=pltpu.VMEM)
SMALL = pltpu.CompilerParams(vmem_limit_bytes=24 * 2**20)
PARTS = 4
PER = SHARDS // PARTS


def put(xs, space):
    return [pltpu.with_memory_space_constraint(x, space) for x in xs]


def copies(pairs, sems):
    return [pltpu.make_async_copy(a, b, sems.at[n]) for n, (a, b) in enumerate(pairs)]


def start(cs):
    for c in cs:
        c.start()


def wait(cs):
    for c in cs:
        c.wait()


def part_of(ref, k):
    size = ref.shape[2] // PARTS
    return ref.at[:, :, pl.ds(k * size, size)]


def lanes(shape):
    return lax.broadcasted_iota(jnp.int32, shape, len(shape) - 1)


def roll(x, shift):
    shift %= 128
    return pltpu.roll(x, shift, x.ndim - 1) if shift else x


def swap_halves(x0, x1):
    low = lanes(x0.shape) < 64
    return jnp.where(low, x0, roll(x1, 64)), jnp.where(low, roll(x0, 64), x1)


def pack_part(first, second, out, k):
    lane = lanes((16, 128))
    base = k * PER
    for n in range(0, PER, 2):
        cols = slice((base + n) * 64, (base + n) * 64 + 128)
        for row, (attn, ffin, _) in ((0, first), (HEAD, second)):
            for pair in range(2):
                x = swap_halves(attn[2 * pair, :, cols], attn[2 * pair + 1, :, cols])
                for c in range(2):
                    out[base + n + c, row + 16 * pair : row + 16 * pair + 16, :] = x[c]
            x = swap_halves(ffin[0, :, cols], ffin[1, :, cols])
            for c in range(2):
                out[base + n + c, row + 32 : row + 72, :] = x[c]
    for n in range(PER):
        e, at = n % 4, (base + n) // 4 * 640 + n % 4 * 128
        last = []
        for row, ffout in ((0, first[2]), (HEAD, second[2])):
            x = ffout[0, :, at : at + 128]
            y = ffout[0, :, at + 128 : at + 256]
            main = jnp.where(lane < 128 - 32 * e, roll(x, -32 * e), roll(y, -32 * e))
            out[base + n, row + 72 : row + 88, :] = main
            last.append(y)
        low = lanes((8, 128))
        tile = jnp.where(low < 32, roll(last[0][0:8], -32 * e), roll(last[0][8:16], 32 - 32 * e))
        other = jnp.where(low < 96, roll(last[1][0:8], 64 - 32 * e), roll(last[1][8:16], 96 - 32 * e))
        out[base + n, 2 * HEAD :, :] = jnp.where(low < 64, tile, other)


def pack_mv_body(*refs):
    hbm, out, buf, packed, sems, out_sems = refs[:6], refs[6], refs[7:13], refs[13], refs[14], refs[15]
    loads = [
        copies([(part_of(a, k), part_of(b, k)) for a, b in zip(hbm, buf, strict=True)], sems.at[k])
        for k in range(PARTS)
    ]
    stores = copies([(packed.at[pl.ds(k * PER, PER)], out.at[pl.ds(k * PER, PER)]) for k in range(PARTS)], out_sems)
    for k in range(PARTS):
        start(loads[k])
    for k in range(PARTS):
        wait(loads[k])
        pack_part(buf[:3], buf[3:], packed, k)
        stores[k].start()
    wait(stores)


def pack_mv(*moments):
    shape = (SHARDS, 2 * HEAD + 8, 128)
    return pl.pallas_call(
        pack_mv_body,
        in_specs=[ANY] * 6,
        out_specs=ANY,
        out_shape=jax.ShapeDtypeStruct(shape, F32),
        scratch_shapes=[pltpu.VMEM(x.shape, F32) for x in moments]
        + [pltpu.VMEM(shape, F32), pltpu.SemaphoreType.DMA((PARTS, 6)), pltpu.SemaphoreType.DMA((PARTS,))],
        name="pack_mv",
    )(*moments)


def k1_body(me, attn, ffin, ffout, o0, o1, o2, o3, turned):
    outs = (o0, o1, o2, o3)
    lane = lanes((8, 128))
    for pair in range(2):
        both = jnp.concatenate([attn[2 * pair], attn[2 * pair + 1]], axis=0)
        turned[pair * 256 : pair * 256 + 256, :] = both.T
    turned[512:1152, :] = jnp.concatenate([ffin[0], ffin[1]], axis=0).T
    turned[1152:1408, :] = ffout[0, 0:128, :].T
    last = jnp.concatenate([ffout[0, 128:160, :], jnp.zeros((96, 256), F32)], axis=0)
    turned[1408:1664, :] = last.T
    for d in range(SPLIT):
        target = lax.rem(me[0] + d, SPLIT)
        for q in range(4):
            place = q * SPLIT + target
            at = pl.multiple_of(place * 16, 16)
            for pair in range(2):
                outs[d][q, 16 * pair : 16 * pair + 16, :] = turned[pl.ds(pair * 256 + at, 16), :]
            outs[d][q, 32:72, :] = turned[pl.ds(512 + pl.multiple_of(place * 40, 8), 40), :]
            outs[d][q, 72:88, :] = turned[pl.ds(1152 + at, 16), :]
            v0 = turned[pl.ds(1408 + at, 8), :]
            v1 = turned[pl.ds(1416 + at, 8), :]
            outs[d][q, 88:96, :] = jnp.where(lane < 32, v0, roll(v1, 32))


def weight_specs():
    return [
        pl.BlockSpec((4, 64, 256), lambda i, *_: (0, 0, i)),
        pl.BlockSpec((2, 64, 640), lambda i, *_: (0, 0, i)),
        pl.BlockSpec((1, 160, 256), lambda i, *_: (0, 0, i)),
    ]


def pack_home(me, attn, ffin, ffout, name):
    return pl.pallas_call(
        k1_body,
        grid_spec=pltpu.PrefetchScalarGridSpec(
            num_scalar_prefetch=1,
            grid=(2,),
            in_specs=weight_specs(),
            out_specs=[pl.BlockSpec((4, ROWS, 128), lambda i, *_: (i, 0, 0))] * 4,
            scratch_shapes=[pltpu.VMEM((1664, 128), F32)],
        ),
        out_shape=[jax.ShapeDtypeStruct((QS, ROWS, 128), F32)] * 4,
        name=name,
    )(me, attn, ffin, ffout)


GROUPS = ((0, 16), (16, 32), (32, 72), (72, 88))
FIRST_SCALE = 1.0 / correct_one
SECOND_SCALE = 1.0 / correct_two


def update_of(grad, first, second, weight):
    first = beta_one * first + (1.0 - beta_one) * grad
    second = beta_two * second + (1.0 - beta_two) * grad * grad
    ratio = first * FIRST_SCALE / (jnp.sqrt(second * SECOND_SCALE) + epsilon)
    return ratio + decay_rate * weight


def square_sum(x):
    return jnp.sum((x * x).reshape(-1, 8, 128), axis=0)


def update_body(*refs):
    me, mv, g_hbm, w_hbm, u_hbm, out = refs[0], refs[1], refs[2:6], refs[6:10], refs[10:14], refs[14]
    g, w, u, sems, out_sems = refs[15:]
    places = [pl.multiple_of(lax.rem(me[0] + SPLIT - d, SPLIT) * QS, QS) for d in range(SPLIT)]
    loads, stores = [], []
    for d, at in enumerate(places):
        block = pl.ds(at, QS)
        pairs = [(g_hbm[d], g.at[block]), (w_hbm[d], w.at[d])]
        loads.append(copies(pairs, sems.at[d]))
        pairs = [(u.at[d], u_hbm[d]), (g.at[block, 0:HEAD], out.at[block, 0:HEAD])]
        stores.append(copies(pairs, out_sems.at[d]))
        start(loads[d])
    last = pltpu.make_async_copy(g.at[:, HEAD:ROWS], out.at[:, HEAD:ROWS], out_sems.at[SPLIT, 0])
    low = lanes((8, 128)) < 64
    totals = (jnp.zeros((8, 128), F32),) * 8
    for d, at in enumerate(places):
        wait(loads[d])

        def chunk(q, totals, at=at, d=d):
            totals = list(totals)
            for n, (lo, hi) in enumerate(GROUPS):
                weight = w[d, q, lo:hi, :]
                grad = g[at + q, lo:hi, :]
                update = update_of(grad, mv[at + q, lo:hi, :], mv[at + q, HEAD + lo : HEAD + hi, :], weight)
                u[d, q, lo:hi, :] = update
                totals[n] += square_sum(update)
                totals[4 + n] += square_sum(weight)
            weight = w[d, q, HEAD:ROWS, :]
            tile = mv[at + q, 2 * HEAD :, :]
            update = update_of(g[at + q, HEAD:ROWS, :], tile, jnp.where(low, roll(tile, 64), 1.0), weight)
            update = jnp.where(low, update, 0.0)
            u[d, q, HEAD:ROWS, :] = update
            totals[3] += update * update
            totals[7] += weight * weight
            return tuple(totals)

        totals = lax.fori_loop(0, QS, chunk, totals)
        start(stores[d])
    total = jnp.concatenate([jnp.sum(x, axis=0, keepdims=True) for x in totals], axis=0)
    fold = total + roll(total, 96)
    lane = lanes((1, 128))
    rows = []
    for matrix in range(7):
        parts = []
        for kind in range(2):
            group = kind * 4 + (3 if matrix == 6 else matrix // 2)
            row = fold[group : group + 1]
            if matrix == 6:
                row = row + roll(row, 64)
            elif matrix % 2:
                row = roll(row, 64)
            parts.append(row)
        rows.append(jnp.where(lane < 96, roll(parts[0], 64), roll(parts[1], 96)))
    rows.append(jnp.zeros((1, 128), F32))
    sums = jnp.concatenate(rows, axis=0)
    for n in range(SHARDS):
        g[n, HEAD:ROWS, :] = jnp.where(low, g[n, HEAD:ROWS, :], sums)
    last.start()
    for s in stores:
        wait(s)
    last.wait()


def make_update(me, mv, gs, ws):
    return pl.pallas_call(
        update_body,
        grid_spec=pltpu.PrefetchScalarGridSpec(
            num_scalar_prefetch=1,
            in_specs=[VSPEC] + [ANY] * 8,
            out_specs=[ANY] * 5,
            scratch_shapes=[
                pltpu.VMEM((SHARDS, ROWS, 128), F32),
                pltpu.VMEM((SPLIT, QS, ROWS, 128), F32),
                pltpu.VMEM((SPLIT, QS, ROWS, 128), F32),
                pltpu.SemaphoreType.DMA((SPLIT, 2)),
                pltpu.SemaphoreType.DMA((SPLIT + 1, 2)),
            ],
        ),
        out_shape=[pltpu.HBM((QS, ROWS, 128), F32)] * 4 + [pltpu.HBM((SHARDS, ROWS, 128), F32)],
        compiler_params=SMALL,
        name="make_update",
    )(me, *put([mv], pltpu.VMEM), *put([*gs, *ws], pltpu.HBM))


def add_body(x, out):
    out[...] = jnp.sum(x[:, HEAD:ROWS, :], axis=0)


def add_sums(x):
    return pl.pallas_call(
        add_body,
        in_specs=[VSPEC],
        out_specs=VSPEC,
        out_shape=jax.ShapeDtypeStruct((8, 128), F32),
        compiler_params=SMALL,
        name="add_sums",
    )(*put([x], pltpu.VMEM))


def moment_part(g, first, second, k):
    def step(n, at, grad):
        first[n][at] = beta_one * first[n][at] + (1.0 - beta_one) * grad
        second[n][at] = beta_two * second[n][at] + (1.0 - beta_two) * grad * grad

    every = slice(None)
    base = k * PER
    for n in range(base, base + PER, 2):
        cols = slice(n * 64, n * 64 + 128)
        for pair in range(2):
            rows = slice(16 * pair, 16 * pair + 16)
            x = swap_halves(g[n, rows, :], g[n + 1, rows, :])
            for a in range(2):
                step(0, (2 * pair + a, every, cols), x[a])
        x = swap_halves(g[n, 32:72, :], g[n + 1, 32:72, :])
        for a in range(2):
            step(1, (a, every, cols), x[a])
    lane = lanes((16, 128))
    for n in range(base, base + PER, 4):
        before = rest = None
        for b in range(5):
            block = roll(g[n + b, 72:88, :], 32 * b) if b < 4 else None
            here = block
            if b > 0:
                here = rest if block is None else jnp.where(lane < 32 * b, rest, block)
                here = jnp.where(lane < 32 * (b - 1), before, here)
            at = n // 4 * 640 + b * 128
            step(2, (0, every, slice(at, at + 128)), here)
            if b < 4:
                before = block
                tile = g[n + b, HEAD:ROWS, :]
                rest = jnp.concatenate([roll(tile, 32 * b), roll(tile, 32 * b - 32)], axis=0)


def moments_body(*refs):
    g, hbm, new, buf, sems, out_sems = refs[0], refs[1:7], refs[7:13], refs[13:19], refs[19], refs[20]
    loads = [
        copies([(part_of(a, k), part_of(b, k)) for a, b in zip(hbm, buf, strict=True)], sems.at[k])
        for k in range(PARTS)
    ]
    stores = [
        copies([(part_of(b, k), part_of(a, k)) for a, b in zip(new, buf, strict=True)], out_sems.at[k])
        for k in range(PARTS)
    ]
    for k in range(PARTS):
        start(loads[k])
    for k in range(PARTS):
        wait(loads[k])
        moment_part(g, buf[:3], buf[3:], k)
        start(stores[k])
    for k in range(PARTS):
        wait(stores[k])


def new_moments(g, *moments):
    return pl.pallas_call(
        moments_body,
        in_specs=[VSPEC] + [ANY] * 6,
        out_specs=[ANY] * 6,
        out_shape=[pltpu.HBM(x.shape, F32) for x in moments],
        scratch_shapes=[pltpu.VMEM(x.shape, F32) for x in moments]
        + [pltpu.SemaphoreType.DMA((PARTS, 6)), pltpu.SemaphoreType.DMA((PARTS, 6))],
        compiler_params=SMALL,
        name="new_moments",
    )(*put([g], pltpu.VMEM), *put(moments, pltpu.HBM))


def k3b_body(me, s0, s1, s2, s3, u0, u1, u2, u3, attn, ffin, ffout, attn2, ffin2, ffout2, trust_out, turned):
    total = (s0[...] + s2[...]) + (s1[...] + s3[...])
    lane = lanes((8, 128))
    update_sq = jnp.sum(jnp.where((lane >= 64) & (lane < 96), total, 0.0), axis=1, keepdims=True)
    weight_sq = jnp.sum(jnp.where(lane >= 96, total, 0.0), axis=1, keepdims=True)
    trust = jnp.sqrt(weight_sq) / (jnp.sqrt(update_sq) + epsilon)
    for n in range(7):
        trust_out[n] = trust[n, 0]
    scale = learn_rate * trust
    here = pl.ds(pl.multiple_of(pl.program_id(0) * 4, 4), 4)
    for d, u in enumerate((u0, u1.at[here], u2.at[here], u3.at[here])):
        source = lax.rem(me[0] + d, SPLIT)
        for q in range(4):
            place = q * SPLIT + source
            at = pl.multiple_of(place * 16, 16)
            for pair in range(2):
                turned[pl.ds(pair * 256 + at, 16), :] = u[q, 16 * pair : 16 * pair + 16, :]
            turned[pl.ds(512 + pl.multiple_of(place * 40, 8), 40), :] = u[q, 32:72, :]
            turned[pl.ds(1152 + at, 16), :] = u[q, 72:88, :]
            tile = u[q, 88:96, :]
            turned[pl.ds(1408 + at, 8), :] = tile
            turned[pl.ds(1416 + at, 8), :] = roll(tile, -32)
    for pair in range(2):
        back = turned[pair * 256 : pair * 256 + 256, :].T
        for a in range(2):
            n = 2 * pair + a
            attn2[n] = attn[n] - scale[n : n + 1] * back[64 * a : 64 * a + 64]
    back = turned[512:1152, :].T
    for a in range(2):
        ffin2[a] = ffin[a] - scale[4 + a : 5 + a] * back[64 * a : 64 * a + 64]
    ffout2[0, 0:128, :] = ffout[0, 0:128, :] - scale[6:7] * turned[1152:1408, :].T
    ffout2[0, 128:160, :] = ffout[0, 128:160, :] - scale[6:7] * turned[1408:1664, :].T[0:32]


def new_weights(me, sums, us, attn, ffin, ffout):
    return pl.pallas_call(
        k3b_body,
        grid_spec=pltpu.PrefetchScalarGridSpec(
            num_scalar_prefetch=1,
            grid=(2,),
            in_specs=[VSPEC] * 4 + [pl.BlockSpec((4, ROWS, 128), lambda i, *_: (i, 0, 0))] + [VSPEC] * 3 + weight_specs(),
            out_specs=weight_specs() + [pl.BlockSpec(memory_space=pltpu.SMEM)],
            scratch_shapes=[pltpu.VMEM((1664, 128), F32)],
        ),
        out_shape=[pltpu.HBM(x.shape, F32) for x in (attn, ffin, ffout)] + [jax.ShapeDtypeStruct((7,), F32)],
        compiler_params=SMALL,
        name="new_weights",
    )(
        me,
        *put(sums, pltpu.VMEM),
        *put(us[:1], pltpu.HBM),
        *put(us[1:], pltpu.VMEM),
        *put([attn, ffin, ffout], pltpu.HBM),
    )


def along(x, shift):
    shift %= SPLIT
    if shift == 0:
        return x
    return lax.ppermute(x, "tensor", [(i, (i + shift) % SPLIT) for i in range(SPLIT)])


def shards(aw, fw, ow, ag, fg, og, am, fm, om, av, fv, ov):
    t = lax.axis_index("tensor").astype(jnp.int32)
    me = t.reshape(1)
    mv = pack_mv(am, fm, om, av, fv, ov)
    mv_here = lax.all_to_all(mv, "shard", split_axis=0, concat_axis=0, tiled=True)
    g = pack_home(me, ag, fg, og, "pack_grads")
    g = [along(g[d], d) for d in range(SPLIT)]
    w = pack_home(me, aw, fw, ow, "pack_weights")
    w = [along(w[d], d) for d in range(SPLIT)]
    *us, grads = make_update(me, mv_here, g, w)
    us = [along(us[d], -d) for d in range(SPLIT)]
    grads = lax.all_to_all(grads, "shard", split_axis=0, concat_axis=0, tiled=True)
    sums = add_sums(grads)
    sums = [along(sums, d) for d in range(SPLIT)]
    moments = new_moments(grads, am, fm, om, av, fv, ov)
    aw2, fw2, ow2, trust = new_weights(me, sums, us, aw, fw, ow)
    return (aw2, fw2, ow2, *moments, trust)


def solution(mesh):
    home = P(None, "shard", "tensor")
    flat = P(None, ("shard", "tensor"), None)
    in_specs = (home,) * 6 + (flat,) * 6
    out_specs = (home,) * 3 + (flat,) * 6 + (P(),)
    return jax.shard_map(shards, mesh=mesh, in_specs=in_specs, out_specs=out_specs, check_vma=False)
```

```python
import jax
import jax.numpy as jnp
from jax import lax
from jax.experimental import pallas as pl
from jax.experimental.pallas import tpu as pltpu
from jax.sharding import PartitionSpec as P

beta_one = 0.9
beta_two = 0.999
step_number = 10.0
correct_one = 1.0 - beta_one**step_number
correct_two = 1.0 - beta_two**step_number
learn_rate = 0.02
decay_rate = 0.1
epsilon = 1e-06

F32 = jnp.float32
SHARDS = 32
SPLIT = 4
QS = SHARDS // SPLIT
HEAD = 88
ROWS = 96


ANY = pl.BlockSpec(memory_space=pl.ANY)
VSPEC = pl.BlockSpec(memory_space=pltpu.VMEM)
SMALL = pltpu.CompilerParams(vmem_limit_bytes=24 * 2**20)
PARTS = 2
PER = SHARDS // PARTS


def put(xs, space):
    return [pltpu.with_memory_space_constraint(x, space) for x in xs]


def copies(pairs, sems):
    return [pltpu.make_async_copy(a, b, sems.at[n]) for n, (a, b) in enumerate(pairs)]


def start(cs):
    for c in cs:
        c.start()


def wait(cs):
    for c in cs:
        c.wait()


def part_of(ref, k):
    size = ref.shape[2] // PARTS
    return ref.at[:, :, pl.ds(k * size, size)]


def lanes(shape):
    return lax.broadcasted_iota(jnp.int32, shape, len(shape) - 1)


def roll(x, shift):
    shift %= 128
    return pltpu.roll(x, shift, x.ndim - 1) if shift else x


def swap_halves(x0, x1):
    low = lanes(x0.shape) < 64
    turned = roll(jnp.where(low, x1, x0), 64)
    return jnp.where(low, x0, turned), jnp.where(low, turned, x1)


def pack_part(first, second, out, k):
    lane = lanes((16, 128))
    base = k * PER
    for n in range(0, PER, 2):
        cols = slice((base + n) * 64, (base + n) * 64 + 128)
        for row, (attn, ffin, _) in ((0, first), (HEAD, second)):
            for pair in range(2):
                x = swap_halves(attn[2 * pair, :, cols], attn[2 * pair + 1, :, cols])
                for c in range(2):
                    out[base + n + c, row + 16 * pair : row + 16 * pair + 16, :] = x[c]
            x = swap_halves(ffin[0, :, cols], ffin[1, :, cols])
            for c in range(2):
                out[base + n + c, row + 32 : row + 72, :] = x[c]
    for n in range(PER):
        e, at = n % 4, (base + n) // 4 * 640 + n % 4 * 128
        last = []
        for row, ffout in ((0, first[2]), (HEAD, second[2])):
            x = ffout[0, :, at : at + 128]
            y = ffout[0, :, at + 128 : at + 256]
            main = jnp.where(lane < 128 - 32 * e, roll(x, -32 * e), roll(y, -32 * e))
            out[base + n, row + 72 : row + 88, :] = main
            last.append(y)
        low = lanes((8, 128))
        tile = jnp.where(low < 32, roll(last[0][0:8], -32 * e), roll(last[0][8:16], 32 - 32 * e))
        other = jnp.where(low < 96, roll(last[1][0:8], 64 - 32 * e), roll(last[1][8:16], 96 - 32 * e))
        out[base + n, 2 * HEAD :, :] = jnp.where(low < 64, tile, other)


def square_sum(x):
    return jnp.sum((x * x).reshape(-1, 8, 128), axis=0)


def turn(attn, ffin, ffout, last, turned):
    for pair in range(2):
        both = jnp.concatenate([attn[2 * pair], attn[2 * pair + 1]], axis=0)
        turned[pair * 512 : pair * 512 + 512, :] = both.T
    turned[1024:2304, :] = jnp.concatenate([ffin[0], ffin[1]], axis=0).T
    turned[2304:2816, :] = ffout[0, 0:128, :].T
    if last is not None:
        turned[2816:3328, :] = last.T


def turned_rows(place):
    small = pl.multiple_of(place * 16, 16)
    large = pl.multiple_of(place * 40, 8)
    return (
        ((0, 16), small),
        ((16, 32), 512 + small),
        ((32, 72), 1024 + large),
        ((72, 88), 2304 + small),
    )


def deal(me, turned, out, whole):
    lane = lanes((8, 128))
    for d in range(SPLIT):
        target = lax.rem(me + d, SPLIT)
        for q in range(QS):
            place = q * SPLIT + target
            for (lo, hi), at in turned_rows(place):
                out[d, q, lo:hi, :] = turned[pl.ds(at, hi - lo), :]
            if whole:
                at = pl.multiple_of(2816 + place * 16, 8)
                v0, v1 = turned[pl.ds(at, 8), :], turned[pl.ds(at + 8, 8), :]
                high = jnp.where(lane < 96, roll(v0, 32), roll(v1, 64))
                low = jnp.where(lane < 32, v0, roll(v1, 32))
                out[d, q, HEAD:ROWS, :] = jnp.where(lane < 64, low, high)


def pack_first_body(*refs):
    me, hbm, grads, weight, out, pieces = refs[0], refs[1:7], refs[7:10], refs[10], refs[11], refs[12:16]
    buf, packed, gbuf, wbuf, turned, dealt = refs[16:22], refs[22], refs[23:26], refs[26], refs[27], refs[28]
    sems, out_sems, grad_sems, piece_sems = refs[29:]
    loads = [
        copies([(part_of(a, k), part_of(b, k)) for a, b in zip(hbm, buf, strict=True)], sems.at[k])
        for k in range(PARTS)
    ]
    pairs = list(zip(grads, gbuf, strict=True)) + [(weight.at[0, 128:160], wbuf)]
    grad_loads = copies(pairs, grad_sems)
    stores = copies([(packed.at[pl.ds(k * PER, PER)], out.at[pl.ds(k * PER, PER)]) for k in range(PARTS)], out_sems)
    piece_stores = copies([(dealt.at[d], pieces[d]) for d in range(SPLIT)], piece_sems)
    for k in range(PARTS):
        start(loads[k])
    start(grad_loads)
    for k in range(PARTS):
        wait(loads[k])
        pack_part(buf[:3], buf[3:], packed, k)
        stores[k].start()
    wait(grad_loads)
    last = jnp.concatenate([gbuf[2][0, 128:160, :], wbuf[...], jnp.zeros((64, 512), F32)], axis=0)
    turn(*gbuf, last, turned)
    deal(me[0], turned, dealt, True)
    start(piece_stores)
    wait(stores)
    wait(piece_stores)


def pack_first(me, moments, grads, weight):
    shape = (SHARDS, 2 * HEAD + 8, 128)
    dma = pltpu.SemaphoreType.DMA
    return pl.pallas_call(
        pack_first_body,
        grid_spec=pltpu.PrefetchScalarGridSpec(
            num_scalar_prefetch=1,
            in_specs=[ANY] * 10,
            out_specs=[ANY, VSPEC] + [ANY] * 3,
            scratch_shapes=[pltpu.VMEM(x.shape, F32) for x in moments]
            + [pltpu.VMEM(shape, F32)]
            + [pltpu.VMEM(x.shape, F32) for x in grads]
            + [
                pltpu.VMEM((32, 512), F32),
                pltpu.VMEM((3328, 128), F32),
                pltpu.VMEM((SPLIT, QS, ROWS, 128), F32),
                dma((PARTS, 6)),
                dma((PARTS,)),
                dma((4,)),
                dma((SPLIT,)),
            ],
        ),
        out_shape=[jax.ShapeDtypeStruct(shape, F32), pltpu.VMEM((QS, ROWS, 128), F32)]
        + [jax.ShapeDtypeStruct((QS, ROWS, 128), F32)] * 3,
        name="pack_first",
    )(me, *moments, *grads, weight)


def pack_weights_body(*refs):
    me, weights, pieces, buf, turned, dealt, sems, piece_sems = refs[0], refs[1:4], refs[4:8], refs[8:11], *refs[11:]
    loads = copies(list(zip(weights, buf, strict=True)), sems)
    piece_stores = copies([(dealt.at[d], pieces[d]) for d in range(SPLIT)], piece_sems)
    start(loads)
    wait(loads)
    turn(*buf, None, turned)
    deal(me[0], turned, dealt, False)
    start(piece_stores)
    wait(piece_stores)


def pack_weights(me, weights):
    return pl.pallas_call(
        pack_weights_body,
        grid_spec=pltpu.PrefetchScalarGridSpec(
            num_scalar_prefetch=1,
            in_specs=[ANY] * 3,
            out_specs=[ANY] * 4,
            scratch_shapes=[pltpu.VMEM(x.shape, F32) for x in weights]
            + [
                pltpu.VMEM((2816, 128), F32),
                pltpu.VMEM((SPLIT, QS, HEAD, 128), F32),
                pltpu.SemaphoreType.DMA((3,)),
                pltpu.SemaphoreType.DMA((SPLIT,)),
            ],
        ),
        out_shape=[jax.ShapeDtypeStruct((QS, HEAD, 128), F32)] * 4,
        name="pack_weights",
    )(me, *weights)


def squares_body(attn, ffin, ffout, out):
    def total(x):
        return sum(square_sum(x[:, n : n + 128]) for n in range(0, x.shape[1], 128))

    low = lanes((8, 128)) < 64
    for n, (x, y) in enumerate(((attn[0], attn[1]), (attn[2], attn[3]), (ffin[0], ffin[1]))):
        x, y = total(x), total(y)
        out[n] = jnp.where(low, x + roll(x, 64), y + roll(y, 64))
    out[3] = total(ffout[0])


def square_weights(weights):
    return pl.pallas_call(
        squares_body,
        in_specs=[pl.BlockSpec()] * 3,
        out_specs=pl.BlockSpec(),
        out_shape=jax.ShapeDtypeStruct((4, 8, 128), F32),
        name="square_weights",
    )(*weights)


def weight_specs():
    return [
        pl.BlockSpec((4, 64, 256), lambda i, *_: (0, 0, i)),
        pl.BlockSpec((2, 64, 640), lambda i, *_: (0, 0, i)),
        pl.BlockSpec((1, 160, 256), lambda i, *_: (0, 0, i)),
    ]


GROUPS = ((0, 16), (16, 32), (32, 72), (72, 88))
FIRST_SCALE = 1.0 / correct_one
SECOND_SCALE = 1.0 / correct_two


def ratio_of(grad, first, second):
    first = beta_one * first + (1.0 - beta_one) * grad
    second = beta_two * second + (1.0 - beta_two) * grad * grad
    return first * FIRST_SCALE / (jnp.sqrt(second * SECOND_SCALE) + epsilon)


def update_body(*refs):
    me, mv, g_own, squares_hbm, g_hbm, w_hbm, u_hbm, out = *refs[0:4], refs[4:7], refs[7:11], refs[11:15], refs[15]
    g, w, u, squares, sems, out_sems = refs[16:]
    places = [pl.multiple_of(lax.rem(me[0] + SPLIT - d, SPLIT) * QS, QS) for d in range(SPLIT)]
    blocks = [pl.ds(at, QS) for at in places]
    grad_loads = [pltpu.make_async_copy(g_hbm[d - 1], g.at[blocks[d]], sems.at[d, 0]) for d in range(1, SPLIT)]
    loads = [pltpu.make_async_copy(w_hbm[d], w.at[d], sems.at[d, 1]) for d in range(SPLIT)]
    heads = copies([(g.at[b, 0:HEAD], out.at[b, 0:HEAD]) for b in blocks], out_sems.at[0])
    stores = copies([(u.at[d], u_hbm[d]) for d in range(SPLIT)], out_sems.at[1])
    last = pltpu.make_async_copy(g.at[:, HEAD:ROWS], out.at[:, HEAD:ROWS], out_sems.at[2, 0])
    square_load = pltpu.make_async_copy(squares_hbm, squares, sems.at[0, 0])
    loads[0].start()
    square_load.start()
    for d in range(1, SPLIT):
        grad_loads[d - 1].start()
        loads[d].start()
    low = lanes((8, 128)) < 64

    def ratio_rows(n, q, at, grad):
        if n < 4:
            lo, hi = GROUPS[n]
            return ratio_of(grad, mv[at + q, lo:hi, :], mv[at + q, HEAD + lo : HEAD + hi, :])
        tile = mv[at + q, 2 * HEAD :, :]
        return jnp.where(low, ratio_of(grad, tile, jnp.where(low, roll(tile, 64), 1.0)), 0.0)

    def own_ratio(q, carry):
        for n, (lo, hi) in enumerate((*GROUPS, (HEAD, ROWS))):
            grad = g_own[q, lo:hi, :]
            g[places[0] + q, lo:hi, :] = grad
            u[0, q, lo:hi, :] = ratio_rows(n, q, places[0], grad)
        return carry

    lax.fori_loop(0, QS, own_ratio, 0, unroll=8)
    totals = (jnp.zeros((8, 128), F32),) * 4
    for d in range(SPLIT):
        if d:
            grad_loads[d - 1].wait()
        heads[d].start()
        loads[d].wait()

        def chunk(q, totals, d=d):
            totals = list(totals)
            at = places[d]
            for n, (lo, hi) in enumerate((*GROUPS, (HEAD, ROWS))):
                grad = g[at + q, lo:hi, :]
                ratio = ratio_rows(n, q, at, grad) if d else u[0, q, lo:hi, :]
                weight = w[d, q, lo:hi, :] if n < 4 else jnp.where(low, roll(grad, 64), 0.0)
                update = ratio + decay_rate * weight
                u[d, q, lo:hi, :] = update
                totals[min(n, 3)] += square_sum(update)
            return tuple(totals)

        totals = lax.fori_loop(0, QS, chunk, totals, unroll=8)
        stores[d].start()
    square_load.wait()
    totals = [*totals, *(squares[n] for n in range(4))]
    total = jnp.concatenate([jnp.sum(x, axis=0, keepdims=True) for x in totals], axis=0)
    fold = total + roll(total, 96)
    lane = lanes((1, 128))
    rows = []
    for matrix in range(7):
        parts = []
        for kind in range(2):
            group = kind * 4 + (3 if matrix == 6 else matrix // 2)
            row = fold[group : group + 1]
            if matrix == 6:
                row = row + roll(row, 64)
            elif matrix % 2:
                row = roll(row, 64)
            parts.append(row)
        rows.append(jnp.where(lane < 96, roll(parts[0], 64), roll(parts[1], 96)))
    rows.append(jnp.zeros((1, 128), F32))
    sums = jnp.concatenate(rows, axis=0)
    for n in range(SHARDS):
        g[n, HEAD:ROWS, :] = jnp.where(low, g[n, HEAD:ROWS, :], sums)
    last.start()
    wait(heads)
    wait(stores)
    last.wait()


def make_update(me, mv, squares, gs, ws):
    return pl.pallas_call(
        update_body,
        grid_spec=pltpu.PrefetchScalarGridSpec(
            num_scalar_prefetch=1,
            in_specs=[VSPEC] * 2 + [ANY] * 8,
            out_specs=[ANY] * 5,
            scratch_shapes=[
                pltpu.VMEM((SHARDS, ROWS, 128), F32),
                pltpu.VMEM((SPLIT, QS, HEAD, 128), F32),
                pltpu.VMEM((SPLIT, QS, ROWS, 128), F32),
                pltpu.VMEM((4, 8, 128), F32),
                pltpu.SemaphoreType.DMA((SPLIT, 2)),
                pltpu.SemaphoreType.DMA((3, SPLIT)),
            ],
        ),
        out_shape=[pltpu.HBM((QS, ROWS, 128), F32)] * 4 + [pltpu.HBM((SHARDS, ROWS, 128), F32)],
        compiler_params=SMALL,
        name="make_update",
    )(me, *put([mv, gs[0]], pltpu.VMEM), *put([squares, *gs[1:], *ws], pltpu.HBM))


def add_body(x, out):
    out[...] = jnp.sum(x[:, HEAD:ROWS, :], axis=0)


def add_sums(x):
    return pl.pallas_call(
        add_body,
        in_specs=[VSPEC],
        out_specs=VSPEC,
        out_shape=jax.ShapeDtypeStruct((8, 128), F32),
        compiler_params=SMALL,
        name="add_sums",
    )(*put([x], pltpu.VMEM))


def moment_part(g, first, second, k):
    def step(n, at, grad):
        first[n][at] = beta_one * first[n][at] + (1.0 - beta_one) * grad
        second[n][at] = beta_two * second[n][at] + (1.0 - beta_two) * grad * grad

    every = slice(None)
    base = k * PER
    for n in range(base, base + PER, 2):
        cols = slice(n * 64, n * 64 + 128)
        for pair in range(2):
            rows = slice(16 * pair, 16 * pair + 16)
            x = swap_halves(g[n, rows, :], g[n + 1, rows, :])
            for a in range(2):
                step(0, (2 * pair + a, every, cols), x[a])
        x = swap_halves(g[n, 32:72, :], g[n + 1, 32:72, :])
        for a in range(2):
            step(1, (a, every, cols), x[a])
    lane = lanes((16, 128))
    for n in range(base, base + PER, 4):
        before = rest = None
        for b in range(5):
            block = roll(g[n + b, 72:88, :], 32 * b) if b < 4 else None
            here = block
            if b > 0:
                here = rest if block is None else jnp.where(lane < 32 * b, rest, block)
                here = jnp.where(lane < 32 * (b - 1), before, here)
            at = n // 4 * 640 + b * 128
            step(2, (0, every, slice(at, at + 128)), here)
            if b < 4:
                before = block
                tile = g[n + b, HEAD:ROWS, :]
                rest = jnp.concatenate([roll(tile, 32 * b), roll(tile, 32 * b - 32)], axis=0)


def moments_body(*refs):
    g, hbm, new, buf, sems, out_sems = refs[0], refs[1:7], refs[7:13], refs[13:19], refs[19], refs[20]
    loads = [
        copies([(part_of(a, k), part_of(b, k)) for a, b in zip(hbm, buf, strict=True)], sems.at[k])
        for k in range(PARTS)
    ]
    stores = [
        copies([(part_of(b, k), part_of(a, k)) for a, b in zip(new, buf, strict=True)], out_sems.at[k])
        for k in range(PARTS)
    ]
    for k in range(PARTS):
        start(loads[k])
    for k in range(PARTS):
        wait(loads[k])
        moment_part(g, buf[:3], buf[3:], k)
        start(stores[k])
    for k in range(PARTS):
        wait(stores[k])


def new_moments(g, *moments):
    return pl.pallas_call(
        moments_body,
        in_specs=[VSPEC] + [ANY] * 6,
        out_specs=[ANY] * 6,
        out_shape=[pltpu.HBM(x.shape, F32) for x in moments],
        scratch_shapes=[pltpu.VMEM(x.shape, F32) for x in moments]
        + [pltpu.SemaphoreType.DMA((PARTS, 6)), pltpu.SemaphoreType.DMA((PARTS, 6))],
        compiler_params=SMALL,
        name="new_moments",
    )(*put([g], pltpu.VMEM), *put(moments, pltpu.HBM))


def k3b_body(me, s0, s1, s2, s3, u0, u1, u2, u3, attn, ffin, ffout, attn2, ffin2, ffout2, trust_out, turned):
    total = (s0[...] + s2[...]) + (s1[...] + s3[...])
    lane = lanes((8, 128))
    update_sq = jnp.sum(jnp.where((lane >= 64) & (lane < 96), total, 0.0), axis=1, keepdims=True)
    weight_sq = jnp.sum(jnp.where(lane >= 96, total, 0.0), axis=1, keepdims=True)
    trust = jnp.sqrt(weight_sq) / (jnp.sqrt(update_sq) + epsilon)
    for n in range(7):
        trust_out[n] = trust[n, 0]
    scale = learn_rate * trust
    here = pl.ds(pl.multiple_of(pl.program_id(0) * 4, 4), 4)
    for d, u in enumerate((u0, u1.at[here], u2.at[here], u3.at[here])):
        source = lax.rem(me[0] + d, SPLIT)
        for q in range(4):
            place = q * SPLIT + source
            at = pl.multiple_of(place * 16, 16)
            for pair in range(2):
                turned[pl.ds(pair * 256 + at, 16), :] = u[q, 16 * pair : 16 * pair + 16, :]
            turned[pl.ds(512 + pl.multiple_of(place * 40, 8), 40), :] = u[q, 32:72, :]
            turned[pl.ds(1152 + at, 16), :] = u[q, 72:88, :]
            tile = u[q, 88:96, :]
            turned[pl.ds(1408 + at, 8), :] = tile
            turned[pl.ds(1416 + at, 8), :] = roll(tile, -32)
    for pair in range(2):
        back = turned[pair * 256 : pair * 256 + 256, :].T
        for a in range(2):
            n = 2 * pair + a
            attn2[n] = attn[n] - scale[n : n + 1] * back[64 * a : 64 * a + 64]
    back = turned[512:1152, :].T
    for a in range(2):
        ffin2[a] = ffin[a] - scale[4 + a : 5 + a] * back[64 * a : 64 * a + 64]
    ffout2[0, 0:128, :] = ffout[0, 0:128, :] - scale[6:7] * turned[1152:1408, :].T
    ffout2[0, 128:160, :] = ffout[0, 128:160, :] - scale[6:7] * turned[1408:1664, :].T[0:32]


def new_weights(me, sums, us, attn, ffin, ffout):
    return pl.pallas_call(
        k3b_body,
        grid_spec=pltpu.PrefetchScalarGridSpec(
            num_scalar_prefetch=1,
            grid=(2,),
            in_specs=[VSPEC] * 4 + [pl.BlockSpec((4, ROWS, 128), lambda i, *_: (i, 0, 0))] + [VSPEC] * 3 + weight_specs(),
            out_specs=weight_specs() + [pl.BlockSpec(memory_space=pltpu.SMEM)],
            scratch_shapes=[pltpu.VMEM((1664, 128), F32)],
        ),
        out_shape=[pltpu.HBM(x.shape, F32) for x in (attn, ffin, ffout)] + [jax.ShapeDtypeStruct((7,), F32)],
        compiler_params=SMALL,
        name="new_weights",
    )(
        me,
        *put(sums, pltpu.VMEM),
        *put(us[:1], pltpu.HBM),
        *put(us[1:], pltpu.VMEM),
        *put([attn, ffin, ffout], pltpu.HBM),
    )


ORDER = (1, 3, 2)


def along(x, shift):
    shift %= SPLIT
    if shift == 0:
        return x
    return lax.ppermute(x, "tensor", [(i, (i + shift) % SPLIT) for i in range(SPLIT)])


def shards(aw, fw, ow, ag, fg, og, am, fm, om, av, fv, ov):
    t = lax.axis_index("tensor").astype(jnp.int32)
    me = t.reshape(1)
    mv, *g = pack_first(me, (am, fm, om, av, fv, ov), (ag, fg, og), ow)
    mv_here = lax.all_to_all(mv, "shard", split_axis=0, concat_axis=0, tiled=True)
    for d in ORDER:
        g[d] = along(g[d], d)
    w = list(pack_weights(me, (aw, fw, ow)))
    for d in ORDER:
        w[d] = along(w[d], d)
    *own, _ = lax.optimization_barrier((aw, fw, ow, g[2]))
    squares = square_weights(own)
    *us, grads = make_update(me, mv_here, squares, g, w)
    us = [along(us[d], -d) for d in range(SPLIT)]
    grads = lax.all_to_all(grads, "shard", split_axis=0, concat_axis=0, tiled=True)
    sums = add_sums(grads)
    sums = [along(sums, d) for d in range(SPLIT)]
    moments = new_moments(grads, am, fm, om, av, fv, ov)
    aw2, fw2, ow2, trust = new_weights(me, sums, us, aw, fw, ow)
    return (aw2, fw2, ow2, *moments, trust)


def solution(mesh):
    home = P(None, "shard", "tensor")
    flat = P(None, ("shard", "tensor"), None)
    in_specs = (home,) * 6 + (flat,) * 6
    out_specs = (home,) * 3 + (flat,) * 6 + (P(),)
    return jax.shard_map(shards, mesh=mesh, in_specs=in_specs, out_specs=out_specs, check_vma=False)
```

```python
import jax
import jax.numpy as jnp
from jax import lax
from jax.experimental import pallas as pl
from jax.experimental.pallas import tpu as pltpu
from jax.sharding import PartitionSpec as P

beta_one = 0.9
beta_two = 0.999
step_number = 10.0
correct_one = 1.0 - beta_one**step_number
correct_two = 1.0 - beta_two**step_number
learn_rate = 0.02
decay_rate = 0.1
epsilon = 1e-06

F32 = jnp.float32
SHARDS = 32
SPLIT = 4
QS = SHARDS // SPLIT
HEAD = 88
ROWS = 96


ANY = pl.BlockSpec(memory_space=pl.ANY)
VSPEC = pl.BlockSpec(memory_space=pltpu.VMEM)
SMALL = pltpu.CompilerParams(vmem_limit_bytes=24 * 2**20)
PARTS = 2
PER = SHARDS // PARTS


def put(xs, space):
    return [pltpu.with_memory_space_constraint(x, space) for x in xs]


def copies(pairs, sems):
    return [pltpu.make_async_copy(a, b, sems.at[n]) for n, (a, b) in enumerate(pairs)]


def start(cs):
    for c in cs:
        c.start()


def wait(cs):
    for c in cs:
        c.wait()


def part_of(ref, k):
    size = ref.shape[2] // PARTS
    return ref.at[:, :, pl.ds(k * size, size)]


def lanes(shape):
    return lax.broadcasted_iota(jnp.int32, shape, len(shape) - 1)


def roll(x, shift):
    shift %= 128
    return pltpu.roll(x, shift, x.ndim - 1) if shift else x


def swap_halves(x0, x1):
    low = lanes(x0.shape) < 64
    turned = roll(jnp.where(low, x1, x0), 64)
    return jnp.where(low, x0, turned), jnp.where(low, turned, x1)


def pack_part(first, second, out, k):
    lane = lanes((16, 128))
    base = k * PER
    for n in range(0, PER, 2):
        cols = slice((base + n) * 64, (base + n) * 64 + 128)
        for row, (attn, ffin, _) in ((0, first), (HEAD, second)):
            for pair in range(2):
                x = swap_halves(attn[2 * pair, :, cols], attn[2 * pair + 1, :, cols])
                for c in range(2):
                    out[base + n + c, row + 16 * pair : row + 16 * pair + 16, :] = x[c]
            x = swap_halves(ffin[0, :, cols], ffin[1, :, cols])
            for c in range(2):
                out[base + n + c, row + 32 : row + 72, :] = x[c]
    for n in range(PER):
        e, at = n % 4, (base + n) // 4 * 640 + n % 4 * 128
        last = []
        for row, ffout in ((0, first[2]), (HEAD, second[2])):
            x = ffout[0, :, at : at + 128]
            y = ffout[0, :, at + 128 : at + 256]
            main = jnp.where(lane < 128 - 32 * e, roll(x, -32 * e), roll(y, -32 * e))
            out[base + n, row + 72 : row + 88, :] = main
            last.append(y)
        low = lanes((8, 128))
        tile = jnp.where(low < 32, roll(last[0][0:8], -32 * e), roll(last[0][8:16], 32 - 32 * e))
        other = jnp.where(low < 96, roll(last[1][0:8], 64 - 32 * e), roll(last[1][8:16], 96 - 32 * e))
        out[base + n, 2 * HEAD :, :] = jnp.where(low < 64, tile, other)


def square_sum(x):
    return jnp.sum((x * x).reshape(-1, 8, 128), axis=0)


def turn(attn, ffin, ffout, last, turned):
    for pair in range(2):
        both = jnp.concatenate([attn[2 * pair], attn[2 * pair + 1]], axis=0)
        turned[pair * 512 : pair * 512 + 512, :] = both.T
    turned[1024:2304, :] = jnp.concatenate([ffin[0], ffin[1]], axis=0).T
    turned[2304:2816, :] = ffout[0, 0:128, :].T
    if last is not None:
        turned[2816:3328, :] = last.T


def turned_rows(place):
    small = pl.multiple_of(place * 16, 16)
    large = pl.multiple_of(place * 40, 8)
    return (
        ((0, 16), small),
        ((16, 32), 512 + small),
        ((32, 72), 1024 + large),
        ((72, 88), 2304 + small),
    )


def deal(me, turned, out, whole):
    lane = lanes((8, 128))
    for d in range(SPLIT):
        target = lax.rem(me + d, SPLIT)
        for q in range(QS):
            place = q * SPLIT + target
            for (lo, hi), at in turned_rows(place):
                out[d, q, lo:hi, :] = turned[pl.ds(at, hi - lo), :]
            if whole:
                at = pl.multiple_of(2816 + place * 16, 8)
                v0, v1 = turned[pl.ds(at, 8), :], turned[pl.ds(at + 8, 8), :]
                high = jnp.where(lane < 96, roll(v0, 32), roll(v1, 64))
                low = jnp.where(lane < 32, v0, roll(v1, 32))
                out[d, q, HEAD:ROWS, :] = jnp.where(lane < 64, low, high)


def pack_first_body(*refs):
    me, hbm, grads, weight, out, pieces = refs[0], refs[1:7], refs[7:10], refs[10], refs[11], refs[12:16]
    buf, packed, gbuf, wbuf, turned, dealt = refs[16:22], refs[22], refs[23:26], refs[26], refs[27], refs[28]
    sems, out_sems, grad_sems, piece_sems = refs[29:]
    loads = [
        copies([(part_of(a, k), part_of(b, k)) for a, b in zip(hbm, buf, strict=True)], sems.at[k])
        for k in range(PARTS)
    ]
    pairs = list(zip(grads, gbuf, strict=True)) + [(weight.at[0, 128:160], wbuf)]
    grad_loads = copies(pairs, grad_sems)
    stores = copies([(packed.at[pl.ds(k * PER, PER)], out.at[pl.ds(k * PER, PER)]) for k in range(PARTS)], out_sems)
    piece_stores = copies([(dealt.at[d], pieces[d]) for d in range(SPLIT)], piece_sems)
    for k in range(PARTS):
        start(loads[k])
    start(grad_loads)
    for k in range(PARTS):
        wait(loads[k])
        pack_part(buf[:3], buf[3:], packed, k)
        stores[k].start()
    wait(grad_loads)
    last = jnp.concatenate([gbuf[2][0, 128:160, :], wbuf[...], jnp.zeros((64, 512), F32)], axis=0)
    turn(*gbuf, last, turned)
    deal(me[0], turned, dealt, True)
    start(piece_stores)
    wait(stores)
    wait(piece_stores)


def pack_first(me, moments, grads, weight):
    shape = (SHARDS, 2 * HEAD + 8, 128)
    dma = pltpu.SemaphoreType.DMA
    return pl.pallas_call(
        pack_first_body,
        grid_spec=pltpu.PrefetchScalarGridSpec(
            num_scalar_prefetch=1,
            in_specs=[ANY] * 10,
            out_specs=[ANY, VSPEC] + [ANY] * 3,
            scratch_shapes=[pltpu.VMEM(x.shape, F32) for x in moments]
            + [pltpu.VMEM(shape, F32)]
            + [pltpu.VMEM(x.shape, F32) for x in grads]
            + [
                pltpu.VMEM((32, 512), F32),
                pltpu.VMEM((3328, 128), F32),
                pltpu.VMEM((SPLIT, QS, ROWS, 128), F32),
                dma((PARTS, 6)),
                dma((PARTS,)),
                dma((4,)),
                dma((SPLIT,)),
            ],
        ),
        out_shape=[jax.ShapeDtypeStruct(shape, F32), pltpu.VMEM((QS, ROWS, 128), F32)]
        + [jax.ShapeDtypeStruct((QS, ROWS, 128), F32)] * 3,
        name="pack_first",
    )(me, *moments, *grads, weight)


def pack_weights_body(*refs):
    me, weights, pieces, buf, turned, dealt, sems, piece_sems = refs[0], refs[1:4], refs[4:8], refs[8:11], *refs[11:]
    loads = copies(list(zip(weights, buf, strict=True)), sems)
    piece_stores = copies([(dealt.at[d], pieces[d]) for d in range(SPLIT)], piece_sems)
    start(loads)
    wait(loads)
    turn(*buf, None, turned)
    deal(me[0], turned, dealt, False)
    start(piece_stores)
    wait(piece_stores)


def pack_weights(me, weights):
    return pl.pallas_call(
        pack_weights_body,
        grid_spec=pltpu.PrefetchScalarGridSpec(
            num_scalar_prefetch=1,
            in_specs=[ANY] * 3,
            out_specs=[ANY] * 4,
            scratch_shapes=[pltpu.VMEM(x.shape, F32) for x in weights]
            + [
                pltpu.VMEM((2816, 128), F32),
                pltpu.VMEM((SPLIT, QS, HEAD, 128), F32),
                pltpu.SemaphoreType.DMA((3,)),
                pltpu.SemaphoreType.DMA((SPLIT,)),
            ],
        ),
        out_shape=[jax.ShapeDtypeStruct((QS, HEAD, 128), F32)] * 4,
        name="pack_weights",
    )(me, *weights)


def gather_body(*refs):
    me, g_own, g_hbm, weights, out, squares_hbm = refs[0], refs[1], refs[2:5], refs[5:8], refs[8], refs[9]
    buf, gbuf, squares, sems, grad_sems, out_sems = refs[10:13], *refs[13:]
    moves = []
    for d, g in enumerate((g_own, *(gbuf.at[n] for n in range(3)))):
        block = pl.ds(pl.multiple_of(lax.rem(me[0] + SPLIT - d, SPLIT) * QS, QS), QS)
        moves.append(pltpu.make_async_copy(g, out.at[block], out_sems.at[d]))
    loads = copies(list(zip(weights, buf, strict=True)), sems)
    grad_loads = copies([(g, gbuf.at[n]) for n, g in enumerate(g_hbm)], grad_sems)
    start(grad_loads)
    start(loads)
    moves[0].start()
    wait(grad_loads)
    start(moves[1:])
    wait(loads)
    attn, ffin, ffout = buf

    def total(x):
        return sum(square_sum(x[:, n : n + 128]) for n in range(0, x.shape[1], 128))

    low = lanes((8, 128)) < 64
    for n, (x, y) in enumerate(((attn[0], attn[1]), (attn[2], attn[3]), (ffin[0], ffin[1]))):
        x, y = total(x), total(y)
        squares[n] = jnp.where(low, x + roll(x, 64), y + roll(y, 64))
    squares[3] = total(ffout[0])
    done = pltpu.make_async_copy(squares, squares_hbm, out_sems.at[SPLIT])
    done.start()
    wait(moves)
    done.wait()


def gather_grads(me, gs, weights):
    return pl.pallas_call(
        gather_body,
        grid_spec=pltpu.PrefetchScalarGridSpec(
            num_scalar_prefetch=1,
            in_specs=[VSPEC] + [ANY] * 6,
            out_specs=[ANY] * 2,
            scratch_shapes=[pltpu.VMEM(x.shape, F32) for x in weights]
            + [
                pltpu.VMEM((3, QS, ROWS, 128), F32),
                pltpu.VMEM((4, 8, 128), F32),
                pltpu.SemaphoreType.DMA((3,)),
                pltpu.SemaphoreType.DMA((3,)),
                pltpu.SemaphoreType.DMA((SPLIT + 1,)),
            ],
        ),
        out_shape=[pltpu.HBM((SHARDS, ROWS, 128), F32), pltpu.HBM((4, 8, 128), F32)],
        name="gather_grads",
    )(me, *put(gs[:1], pltpu.VMEM), *put([*gs[1:], *weights], pltpu.HBM))


def weight_specs():
    return [
        pl.BlockSpec((4, 64, 256), lambda i, *_: (0, 0, i)),
        pl.BlockSpec((2, 64, 640), lambda i, *_: (0, 0, i)),
        pl.BlockSpec((1, 160, 256), lambda i, *_: (0, 0, i)),
    ]


GROUPS = ((0, 16), (16, 32), (32, 72), (72, 88))
FIRST_SCALE = 1.0 / correct_one
SECOND_SCALE = 1.0 / correct_two


def ratio_of(grad, first, second):
    first = beta_one * first + (1.0 - beta_one) * grad
    second = beta_two * second + (1.0 - beta_two) * grad * grad
    return first * FIRST_SCALE / (jnp.sqrt(second * SECOND_SCALE) + epsilon)


def update_body(*refs):
    me, mv, g_own, squares_hbm, g_hbm, w_hbm, u_hbm, out = *refs[0:5], refs[5:9], refs[9:13], refs[13]
    g, w, u, squares, sems, out_sems = refs[14:]
    places = [pl.multiple_of(lax.rem(me[0] + SPLIT - d, SPLIT) * QS, QS) for d in range(SPLIT)]
    blocks = [pl.ds(at, QS) for at in places]
    grad_loads = [pltpu.make_async_copy(g_hbm.at[b], g.at[b], sems.at[d, 0]) for d, b in enumerate(blocks) if d]
    loads = [pltpu.make_async_copy(w_hbm[d], w.at[d], sems.at[d, 1]) for d in range(SPLIT)]
    stores = copies([(u.at[d], u_hbm[d]) for d in range(SPLIT)], out_sems)
    last = pltpu.make_async_copy(g.at[:, HEAD:ROWS], out.at[:, HEAD:ROWS], out_sems.at[SPLIT])
    square_load = pltpu.make_async_copy(squares_hbm, squares, sems.at[0, 0])
    loads[0].start()
    for d in range(1, SPLIT):
        grad_loads[d - 1].start()
        loads[d].start()
    square_load.start()
    low = lanes((8, 128)) < 64

    def ratio_rows(n, q, at, grad):
        if n < 4:
            lo, hi = GROUPS[n]
            return ratio_of(grad, mv[at + q, lo:hi, :], mv[at + q, HEAD + lo : HEAD + hi, :])
        tile = mv[at + q, 2 * HEAD :, :]
        return jnp.where(low, ratio_of(grad, tile, jnp.where(low, roll(tile, 64), 1.0)), 0.0)

    def own_ratio(q, carry):
        for n, (lo, hi) in enumerate((*GROUPS, (HEAD, ROWS))):
            grad = g_own[q, lo:hi, :]
            if n == 4:
                g[places[0] + q, lo:hi, :] = grad
            u[0, q, lo:hi, :] = ratio_rows(n, q, places[0], grad)
        return carry

    lax.fori_loop(0, QS, own_ratio, 0, unroll=8)
    totals = (jnp.zeros((8, 128), F32),) * 4
    for d in range(SPLIT):
        if d:
            grad_loads[d - 1].wait()
        loads[d].wait()

        def chunk(q, totals, d=d):
            totals = list(totals)
            at = places[d]
            for n, (lo, hi) in enumerate((*GROUPS, (HEAD, ROWS))):
                if d or n == 4:
                    grad = g[at + q, lo:hi, :]
                ratio = ratio_rows(n, q, at, grad) if d else u[0, q, lo:hi, :]
                weight = w[d, q, lo:hi, :] if n < 4 else jnp.where(low, roll(grad, 64), 0.0)
                update = ratio + decay_rate * weight
                u[d, q, lo:hi, :] = update
                totals[min(n, 3)] += square_sum(update)
            return tuple(totals)

        totals = lax.fori_loop(0, QS, chunk, totals, unroll=8)
        stores[d].start()
    square_load.wait()
    totals = [*totals, *(squares[n] for n in range(4))]
    total = jnp.concatenate([jnp.sum(x, axis=0, keepdims=True) for x in totals], axis=0)
    fold = total + roll(total, 96)
    lane = lanes((1, 128))
    rows = []
    for matrix in range(7):
        parts = []
        for kind in range(2):
            group = kind * 4 + (3 if matrix == 6 else matrix // 2)
            row = fold[group : group + 1]
            if matrix == 6:
                row = row + roll(row, 64)
            elif matrix % 2:
                row = roll(row, 64)
            parts.append(row)
        rows.append(jnp.where(lane < 96, roll(parts[0], 64), roll(parts[1], 96)))
    rows.append(jnp.zeros((1, 128), F32))
    sums = jnp.concatenate(rows, axis=0)
    for n in range(SHARDS):
        g[n, HEAD:ROWS, :] = jnp.where(low, g[n, HEAD:ROWS, :], sums)
    last.start()
    wait(stores)
    last.wait()


def make_update(me, mv, own, squares, grads, ws):
    return pl.pallas_call(
        update_body,
        grid_spec=pltpu.PrefetchScalarGridSpec(
            num_scalar_prefetch=1,
            in_specs=[VSPEC] * 2 + [ANY] * 6,
            out_specs=[ANY] * 5,
            scratch_shapes=[
                pltpu.VMEM((SHARDS, ROWS, 128), F32),
                pltpu.VMEM((SPLIT, QS, HEAD, 128), F32),
                pltpu.VMEM((SPLIT, QS, ROWS, 128), F32),
                pltpu.VMEM((4, 8, 128), F32),
                pltpu.SemaphoreType.DMA((SPLIT, 2)),
                pltpu.SemaphoreType.DMA((SPLIT + 1,)),
            ],
        ),
        out_shape=[pltpu.HBM((QS, ROWS, 128), F32)] * 4 + [pltpu.HBM((SHARDS, ROWS, 128), F32)],
        input_output_aliases={4: 4},
        compiler_params=SMALL,
        name="make_update",
    )(me, *put([mv, own], pltpu.VMEM), *put([squares, grads, *ws], pltpu.HBM))


def add_body(x, out):
    out[...] = jnp.sum(x[:, HEAD:ROWS, :], axis=0)


def add_sums(x):
    return pl.pallas_call(
        add_body,
        in_specs=[VSPEC],
        out_specs=VSPEC,
        out_shape=jax.ShapeDtypeStruct((8, 128), F32),
        compiler_params=SMALL,
        name="add_sums",
    )(*put([x], pltpu.VMEM))


def moment_part(g, first, second, k):
    def step(n, at, grad):
        first[n][at] = beta_one * first[n][at] + (1.0 - beta_one) * grad
        second[n][at] = beta_two * second[n][at] + (1.0 - beta_two) * grad * grad

    every = slice(None)
    base = k * PER
    for n in range(base, base + PER, 2):
        cols = slice(n * 64, n * 64 + 128)
        for pair in range(2):
            rows = slice(16 * pair, 16 * pair + 16)
            x = swap_halves(g[n, rows, :], g[n + 1, rows, :])
            for a in range(2):
                step(0, (2 * pair + a, every, cols), x[a])
        x = swap_halves(g[n, 32:72, :], g[n + 1, 32:72, :])
        for a in range(2):
            step(1, (a, every, cols), x[a])
    lane = lanes((16, 128))
    for n in range(base, base + PER, 4):
        before = rest = None
        for b in range(5):
            block = roll(g[n + b, 72:88, :], 32 * b) if b < 4 else None
            here = block
            if b > 0:
                here = rest if block is None else jnp.where(lane < 32 * b, rest, block)
                here = jnp.where(lane < 32 * (b - 1), before, here)
            at = n // 4 * 640 + b * 128
            step(2, (0, every, slice(at, at + 128)), here)
            if b < 4:
                before = block
                tile = g[n + b, HEAD:ROWS, :]
                rest = jnp.concatenate([roll(tile, 32 * b), roll(tile, 32 * b - 32)], axis=0)


def moments_body(*refs):
    g, hbm, new, buf, sems, out_sems = refs[0], refs[1:7], refs[7:13], refs[13:19], refs[19], refs[20]
    loads = [
        copies([(part_of(a, k), part_of(b, k)) for a, b in zip(hbm, buf, strict=True)], sems.at[k])
        for k in range(PARTS)
    ]
    stores = [
        copies([(part_of(b, k), part_of(a, k)) for a, b in zip(new, buf, strict=True)], out_sems.at[k])
        for k in range(PARTS)
    ]
    for k in range(PARTS):
        start(loads[k])
    for k in range(PARTS):
        wait(loads[k])
        moment_part(g, buf[:3], buf[3:], k)
        start(stores[k])
    for k in range(PARTS):
        wait(stores[k])


def new_moments(g, *moments):
    return pl.pallas_call(
        moments_body,
        in_specs=[VSPEC] + [ANY] * 6,
        out_specs=[ANY] * 6,
        out_shape=[pltpu.HBM(x.shape, F32) for x in moments],
        scratch_shapes=[pltpu.VMEM(x.shape, F32) for x in moments]
        + [pltpu.SemaphoreType.DMA((PARTS, 6)), pltpu.SemaphoreType.DMA((PARTS, 6))],
        compiler_params=SMALL,
        name="new_moments",
    )(*put([g], pltpu.VMEM), *put(moments, pltpu.HBM))


def k3b_body(me, s0, s1, s2, s3, u0, u1, u2, u3, attn, ffin, ffout, attn2, ffin2, ffout2, trust_out, turned):
    total = (s0[...] + s2[...]) + (s1[...] + s3[...])
    lane = lanes((8, 128))
    update_sq = jnp.sum(jnp.where((lane >= 64) & (lane < 96), total, 0.0), axis=1, keepdims=True)
    weight_sq = jnp.sum(jnp.where(lane >= 96, total, 0.0), axis=1, keepdims=True)
    trust = jnp.sqrt(weight_sq) / (jnp.sqrt(update_sq) + epsilon)
    for n in range(7):
        trust_out[n] = trust[n, 0]
    scale = learn_rate * trust
    here = pl.ds(pl.multiple_of(pl.program_id(0) * 4, 4), 4)
    for d, u in enumerate((u0, u1.at[here], u2.at[here], u3.at[here])):
        source = lax.rem(me[0] + d, SPLIT)
        for q in range(4):
            place = q * SPLIT + source
            at = pl.multiple_of(place * 16, 16)
            for pair in range(2):
                turned[pl.ds(pair * 256 + at, 16), :] = u[q, 16 * pair : 16 * pair + 16, :]
            turned[pl.ds(512 + pl.multiple_of(place * 40, 8), 40), :] = u[q, 32:72, :]
            turned[pl.ds(1152 + at, 16), :] = u[q, 72:88, :]
            tile = u[q, 88:96, :]
            turned[pl.ds(1408 + at, 8), :] = tile
            turned[pl.ds(1416 + at, 8), :] = roll(tile, -32)
    for pair in range(2):
        back = turned[pair * 256 : pair * 256 + 256, :].T
        for a in range(2):
            n = 2 * pair + a
            attn2[n] = attn[n] - scale[n : n + 1] * back[64 * a : 64 * a + 64]
    back = turned[512:1152, :].T
    for a in range(2):
        ffin2[a] = ffin[a] - scale[4 + a : 5 + a] * back[64 * a : 64 * a + 64]
    ffout2[0, 0:128, :] = ffout[0, 0:128, :] - scale[6:7] * turned[1152:1408, :].T
    ffout2[0, 128:160, :] = ffout[0, 128:160, :] - scale[6:7] * turned[1408:1664, :].T[0:32]


def new_weights(me, sums, us, attn, ffin, ffout):
    return pl.pallas_call(
        k3b_body,
        grid_spec=pltpu.PrefetchScalarGridSpec(
            num_scalar_prefetch=1,
            grid=(2,),
            in_specs=[VSPEC] * 4 + [pl.BlockSpec((4, ROWS, 128), lambda i, *_: (i, 0, 0))] + [VSPEC] * 3 + weight_specs(),
            out_specs=weight_specs() + [pl.BlockSpec(memory_space=pltpu.SMEM)],
            scratch_shapes=[pltpu.VMEM((1664, 128), F32)],
        ),
        out_shape=[pltpu.HBM(x.shape, F32) for x in (attn, ffin, ffout)] + [jax.ShapeDtypeStruct((7,), F32)],
        compiler_params=SMALL,
        name="new_weights",
    )(
        me,
        *put(sums, pltpu.VMEM),
        *put(us[:1], pltpu.HBM),
        *put(us[1:], pltpu.VMEM),
        *put([attn, ffin, ffout], pltpu.HBM),
    )


ORDER = (1, 3, 2)


def along(x, shift):
    shift %= SPLIT
    if shift == 0:
        return x
    return lax.ppermute(x, "tensor", [(i, (i + shift) % SPLIT) for i in range(SPLIT)])


def shards(aw, fw, ow, ag, fg, og, am, fm, om, av, fv, ov):
    t = lax.axis_index("tensor").astype(jnp.int32)
    me = t.reshape(1)
    mv, *g = pack_first(me, (am, fm, om, av, fv, ov), (ag, fg, og), ow)
    mv_here = lax.all_to_all(mv, "shard", split_axis=0, concat_axis=0, tiled=True)
    for d in ORDER:
        g[d] = along(g[d], d)
    w = list(pack_weights(me, (aw, fw, ow)))
    for d in ORDER:
        w[d] = along(w[d], d)
    grads, squares = gather_grads(me, g, (aw, fw, ow))
    *us, grads = make_update(me, mv_here, g[0], squares, grads, w)
    us = list(us)
    for d in (2, 1, 3):
        us[d] = along(us[d], -d)
    grads = lax.all_to_all(grads, "shard", split_axis=0, concat_axis=0, tiled=True)
    sums = add_sums(grads)
    sums = [along(sums, d) for d in range(SPLIT)]
    moments = new_moments(grads, am, fm, om, av, fv, ov)
    aw2, fw2, ow2, trust = new_weights(me, sums, us, aw, fw, ow)
    return (aw2, fw2, ow2, *moments, trust)


def solution(mesh):
    home = P(None, "shard", "tensor")
    flat = P(None, ("shard", "tensor"), None)
    in_specs = (home,) * 6 + (flat,) * 6
    out_specs = (home,) * 3 + (flat,) * 6 + (P(),)
    return jax.shard_map(shards, mesh=mesh, in_specs=in_specs, out_specs=out_specs, check_vma=False)
```

```python
import jax
import jax.numpy as jnp
from jax import lax
from jax.experimental import pallas as pl
from jax.experimental.pallas import tpu as pltpu
from jax.sharding import PartitionSpec as P

beta_one = 0.9
beta_two = 0.999
step_number = 10.0
correct_one = 1.0 - beta_one**step_number
correct_two = 1.0 - beta_two**step_number
learn_rate = 0.02
decay_rate = 0.1
epsilon = 1e-06

F32 = jnp.float32
SHARDS = 32
SPLIT = 4
QS = SHARDS // SPLIT
HEAD = 88
ROWS = 96


ANY = pl.BlockSpec(memory_space=pl.ANY)
VSPEC = pl.BlockSpec(memory_space=pltpu.VMEM)
SMALL = pltpu.CompilerParams(vmem_limit_bytes=24 * 2**20)
PARTS = 2
PER = SHARDS // PARTS


def put(xs, space):
    return [pltpu.with_memory_space_constraint(x, space) for x in xs]


def copies(pairs, sems):
    return [pltpu.make_async_copy(a, b, sems.at[n]) for n, (a, b) in enumerate(pairs)]


def start(cs):
    for c in cs:
        c.start()


def wait(cs):
    for c in cs:
        c.wait()


def part_of(ref, k):
    size = ref.shape[2] // PARTS
    return ref.at[:, :, pl.ds(k * size, size)]


def lanes(shape):
    return lax.broadcasted_iota(jnp.int32, shape, len(shape) - 1)


def roll(x, shift):
    shift %= 128
    return pltpu.roll(x, shift, x.ndim - 1) if shift else x


def swap_halves(x0, x1):
    low = lanes(x0.shape) < 64
    turned = roll(jnp.where(low, x1, x0), 64)
    return jnp.where(low, x0, turned), jnp.where(low, turned, x1)


def pack_part(first, second, out, k):
    lane = lanes((16, 128))
    base = k * PER
    for n in range(0, PER, 2):
        cols = slice((base + n) * 64, (base + n) * 64 + 128)
        for row, (attn, ffin, _) in ((0, first), (HEAD, second)):
            for pair in range(2):
                x = swap_halves(attn[2 * pair, :, cols], attn[2 * pair + 1, :, cols])
                for c in range(2):
                    out[base + n + c, row + 16 * pair : row + 16 * pair + 16, :] = x[c]
            x = swap_halves(ffin[0, :, cols], ffin[1, :, cols])
            for c in range(2):
                out[base + n + c, row + 32 : row + 72, :] = x[c]
    for n in range(PER):
        e, at = n % 4, (base + n) // 4 * 640 + n % 4 * 128
        last = []
        for row, ffout in ((0, first[2]), (HEAD, second[2])):
            x = ffout[0, :, at : at + 128]
            y = ffout[0, :, at + 128 : at + 256]
            main = jnp.where(lane < 128 - 32 * e, roll(x, -32 * e), roll(y, -32 * e))
            out[base + n, row + 72 : row + 88, :] = main
            last.append(y)
        low = lanes((8, 128))
        tile = jnp.where(low < 32, roll(last[0][0:8], -32 * e), roll(last[0][8:16], 32 - 32 * e))
        other = jnp.where(low < 96, roll(last[1][0:8], 64 - 32 * e), roll(last[1][8:16], 96 - 32 * e))
        out[base + n, 2 * HEAD :, :] = jnp.where(low < 64, tile, other)


def square_sum(x):
    return jnp.sum((x * x).reshape(-1, 8, 128), axis=0)


def turn(attn, ffin, ffout, last, turned):
    for pair in range(2):
        both = jnp.concatenate([attn[2 * pair], attn[2 * pair + 1]], axis=0)
        turned[pair * 512 : pair * 512 + 512, :] = both.T
    turned[1024:2304, :] = jnp.concatenate([ffin[0], ffin[1]], axis=0).T
    turned[2304:2816, :] = ffout[0, 0:128, :].T
    if last is not None:
        turned[2816:3328, :] = last.T


def turned_rows(place):
    small = pl.multiple_of(place * 16, 16)
    large = pl.multiple_of(place * 40, 8)
    return (
        ((0, 16), small),
        ((16, 32), 512 + small),
        ((32, 72), 1024 + large),
        ((72, 88), 2304 + small),
    )


def deal(me, turned, out, whole):
    lane = lanes((8, 128))
    for d in range(SPLIT):
        target = lax.rem(me + d, SPLIT)
        for q in range(QS):
            place = q * SPLIT + target
            for (lo, hi), at in turned_rows(place):
                out[d, q, lo:hi, :] = turned[pl.ds(at, hi - lo), :]
            if whole:
                at = pl.multiple_of(2816 + place * 16, 8)
                v0, v1 = turned[pl.ds(at, 8), :], turned[pl.ds(at + 8, 8), :]
                high = jnp.where(lane < 96, roll(v0, 32), roll(v1, 64))
                low = jnp.where(lane < 32, v0, roll(v1, 32))
                out[d, q, HEAD:ROWS, :] = jnp.where(lane < 64, low, high)


def pack_first_body(*refs):
    me, hbm, grads, weight, out, pieces = refs[0], refs[1:7], refs[7:10], refs[10], refs[11], refs[12:16]
    buf, packed, gbuf, wbuf, turned, dealt = refs[16:22], refs[22], refs[23:26], refs[26], refs[27], refs[28]
    sems, out_sems, grad_sems, piece_sems = refs[29:]
    loads = [
        copies([(part_of(a, k), part_of(b, k)) for a, b in zip(hbm, buf, strict=True)], sems.at[k])
        for k in range(PARTS)
    ]
    pairs = list(zip(grads, gbuf, strict=True)) + [(weight.at[0, 128:160], wbuf)]
    grad_loads = copies(pairs, grad_sems)
    stores = copies([(packed.at[pl.ds(k * PER, PER)], out.at[pl.ds(k * PER, PER)]) for k in range(PARTS)], out_sems)
    piece_stores = copies([(dealt.at[d], pieces[d]) for d in range(SPLIT)], piece_sems)
    for k in range(PARTS):
        start(loads[k])
    start(grad_loads)
    for k in range(PARTS):
        wait(loads[k])
        pack_part(buf[:3], buf[3:], packed, k)
        stores[k].start()
    wait(grad_loads)
    last = jnp.concatenate([gbuf[2][0, 128:160, :], wbuf[...], jnp.zeros((64, 512), F32)], axis=0)
    turn(*gbuf, last, turned)
    deal(me[0], turned, dealt, True)
    start(piece_stores)
    wait(stores)
    wait(piece_stores)


def pack_first(me, moments, grads, weight):
    shape = (SHARDS, 2 * HEAD + 8, 128)
    dma = pltpu.SemaphoreType.DMA
    return pl.pallas_call(
        pack_first_body,
        grid_spec=pltpu.PrefetchScalarGridSpec(
            num_scalar_prefetch=1,
            in_specs=[ANY] * 10,
            out_specs=[ANY, VSPEC] + [ANY] * 3,
            scratch_shapes=[pltpu.VMEM(x.shape, F32) for x in moments]
            + [pltpu.VMEM(shape, F32)]
            + [pltpu.VMEM(x.shape, F32) for x in grads]
            + [
                pltpu.VMEM((32, 512), F32),
                pltpu.VMEM((3328, 128), F32),
                pltpu.VMEM((SPLIT, QS, ROWS, 128), F32),
                dma((PARTS, 6)),
                dma((PARTS,)),
                dma((4,)),
                dma((SPLIT,)),
            ],
        ),
        out_shape=[jax.ShapeDtypeStruct(shape, F32), pltpu.VMEM((QS, ROWS, 128), F32)]
        + [jax.ShapeDtypeStruct((QS, ROWS, 128), F32)] * 3,
        name="pack_first",
    )(me, *moments, *grads, weight)


def pack_weights_body(*refs):
    me, weights, pieces, buf, turned, dealt, sems, piece_sems = refs[0], refs[1:4], refs[4:8], refs[8:11], *refs[11:]
    loads = copies(list(zip(weights, buf, strict=True)), sems)
    piece_stores = copies([(dealt.at[d], pieces[d]) for d in range(SPLIT)], piece_sems)
    start(loads)
    wait(loads)
    turn(*buf, None, turned)
    deal(me[0], turned, dealt, False)
    start(piece_stores)
    wait(piece_stores)


def pack_weights(me, weights):
    return pl.pallas_call(
        pack_weights_body,
        grid_spec=pltpu.PrefetchScalarGridSpec(
            num_scalar_prefetch=1,
            in_specs=[ANY] * 3,
            out_specs=[ANY] * 4,
            scratch_shapes=[pltpu.VMEM(x.shape, F32) for x in weights]
            + [
                pltpu.VMEM((2816, 128), F32),
                pltpu.VMEM((SPLIT, QS, HEAD, 128), F32),
                pltpu.SemaphoreType.DMA((3,)),
                pltpu.SemaphoreType.DMA((SPLIT,)),
            ],
        ),
        out_shape=[jax.ShapeDtypeStruct((QS, HEAD, 128), F32)] * 4,
        name="pack_weights",
    )(me, *weights)


def gather_body(*refs):
    me, g_own, g_hbm, weights, out, squares_hbm = refs[0], refs[1], refs[2:5], refs[5:8], refs[8], refs[9]
    buf, gbuf, squares, sems, grad_sems, out_sems = refs[10:13], *refs[13:]
    moves = []
    for d, g in enumerate((g_own, *(gbuf.at[n] for n in range(3)))):
        block = pl.ds(pl.multiple_of(lax.rem(me[0] + SPLIT - d, SPLIT) * QS, QS), QS)
        moves.append(pltpu.make_async_copy(g, out.at[block], out_sems.at[d]))
    loads = copies(list(zip(weights, buf, strict=True)), sems)
    grad_loads = copies([(g, gbuf.at[n]) for n, g in enumerate(g_hbm)], grad_sems)
    start(grad_loads)
    start(loads)
    moves[0].start()
    wait(grad_loads)
    start(moves[1:])
    wait(loads)
    attn, ffin, ffout = buf

    def total(x):
        return sum(square_sum(x[:, n : n + 128]) for n in range(0, x.shape[1], 128))

    low = lanes((8, 128)) < 64
    for n, (x, y) in enumerate(((attn[0], attn[1]), (attn[2], attn[3]), (ffin[0], ffin[1]))):
        x, y = total(x), total(y)
        squares[n] = jnp.where(low, x + roll(x, 64), y + roll(y, 64))
    squares[3] = total(ffout[0])
    done = pltpu.make_async_copy(squares, squares_hbm, out_sems.at[SPLIT])
    done.start()
    wait(moves)
    done.wait()


def gather_grads(me, gs, weights):
    return pl.pallas_call(
        gather_body,
        grid_spec=pltpu.PrefetchScalarGridSpec(
            num_scalar_prefetch=1,
            in_specs=[VSPEC] + [ANY] * 6,
            out_specs=[ANY] * 2,
            scratch_shapes=[pltpu.VMEM(x.shape, F32) for x in weights]
            + [
                pltpu.VMEM((3, QS, ROWS, 128), F32),
                pltpu.VMEM((4, 8, 128), F32),
                pltpu.SemaphoreType.DMA((3,)),
                pltpu.SemaphoreType.DMA((3,)),
                pltpu.SemaphoreType.DMA((SPLIT + 1,)),
            ],
        ),
        out_shape=[pltpu.HBM((SHARDS, ROWS, 128), F32), pltpu.HBM((4, 8, 128), F32)],
        name="gather_grads",
    )(me, *put(gs[:1], pltpu.VMEM), *put([*gs[1:], *weights], pltpu.HBM))


def weight_specs():
    return [
        pl.BlockSpec((4, 64, 256), lambda i, *_: (0, 0, i)),
        pl.BlockSpec((2, 64, 640), lambda i, *_: (0, 0, i)),
        pl.BlockSpec((1, 160, 256), lambda i, *_: (0, 0, i)),
    ]


GROUPS = ((0, 16), (16, 32), (32, 72), (72, 88))
FIRST_SCALE = 1.0 / correct_one
SECOND_SCALE = 1.0 / correct_two


def ratio_of(grad, first, second):
    first = beta_one * first + (1.0 - beta_one) * grad
    second = beta_two * second + (1.0 - beta_two) * grad * grad
    return first * FIRST_SCALE / (jnp.sqrt(second * SECOND_SCALE) + epsilon)


def update_body(*refs):
    me, mv, g_own, squares_hbm, g_hbm, w_hbm, u_hbm, out = *refs[0:5], refs[5:9], refs[9:13], refs[13]
    g, w, u, squares, sems, out_sems = refs[14:]
    places = [pl.multiple_of(lax.rem(me[0] + SPLIT - d, SPLIT) * QS, QS) for d in range(SPLIT)]
    blocks = [pl.ds(at, QS) for at in places]
    grad_loads = [pltpu.make_async_copy(g_hbm.at[b], g.at[b], sems.at[d, 0]) for d, b in enumerate(blocks) if d]
    loads = [pltpu.make_async_copy(w_hbm[d], w.at[d], sems.at[d, 1]) for d in range(SPLIT)]
    stores = copies([(u.at[d], u_hbm[d]) for d in range(SPLIT)], out_sems)
    last = pltpu.make_async_copy(g.at[:, HEAD:ROWS], out.at[:, HEAD:ROWS], out_sems.at[SPLIT])
    square_load = pltpu.make_async_copy(squares_hbm, squares, sems.at[0, 0])
    loads[0].start()
    for d in range(1, SPLIT):
        grad_loads[d - 1].start()
        loads[d].start()
    square_load.start()
    low = lanes((8, 128)) < 64

    def ratio_rows(n, q, at, grad):
        if n < 4:
            lo, hi = GROUPS[n]
            return ratio_of(grad, mv[at + q, lo:hi, :], mv[at + q, HEAD + lo : HEAD + hi, :])
        tile = mv[at + q, 2 * HEAD :, :]
        return jnp.where(low, ratio_of(grad, tile, jnp.where(low, roll(tile, 64), 1.0)), 0.0)

    def own_ratio(q, carry):
        for n, (lo, hi) in enumerate((*GROUPS, (HEAD, ROWS))):
            grad = g_own[q, lo:hi, :]
            if n == 4:
                g[places[0] + q, lo:hi, :] = grad
            u[0, q, lo:hi, :] = ratio_rows(n, q, places[0], grad)
        return carry

    lax.fori_loop(0, QS, own_ratio, 0, unroll=8)
    totals = (jnp.zeros((8, 128), F32),) * 4
    for d in range(SPLIT):
        if d:
            grad_loads[d - 1].wait()
        loads[d].wait()

        def chunk(q, totals, d=d):
            totals = list(totals)
            at = places[d]
            for n, (lo, hi) in enumerate((*GROUPS, (HEAD, ROWS))):
                if d or n == 4:
                    grad = g[at + q, lo:hi, :]
                ratio = ratio_rows(n, q, at, grad) if d else u[0, q, lo:hi, :]
                weight = w[d, q, lo:hi, :] if n < 4 else jnp.where(low, roll(grad, 64), 0.0)
                update = ratio + decay_rate * weight
                u[d, q, lo:hi, :] = update
                totals[min(n, 3)] += square_sum(update)
            return tuple(totals)

        totals = lax.fori_loop(0, QS, chunk, totals, unroll=8)
        stores[d].start()
    square_load.wait()
    totals = [*totals, *(squares[n] for n in range(4))]
    total = jnp.concatenate([jnp.sum(x, axis=0, keepdims=True) for x in totals], axis=0)
    fold = total + roll(total, 96)
    lane = lanes((1, 128))
    rows = []
    for matrix in range(7):
        parts = []
        for kind in range(2):
            group = kind * 4 + (3 if matrix == 6 else matrix // 2)
            row = fold[group : group + 1]
            if matrix == 6:
                row = row + roll(row, 64)
            elif matrix % 2:
                row = roll(row, 64)
            parts.append(row)
        rows.append(jnp.where(lane < 96, roll(parts[0], 64), roll(parts[1], 96)))
    rows.append(jnp.zeros((1, 128), F32))
    sums = jnp.concatenate(rows, axis=0)
    for n in range(SHARDS):
        g[n, HEAD:ROWS, :] = jnp.where(low, g[n, HEAD:ROWS, :], sums)
    last.start()
    wait(stores)
    last.wait()


def make_update(me, mv, own, squares, grads, ws):
    return pl.pallas_call(
        update_body,
        grid_spec=pltpu.PrefetchScalarGridSpec(
            num_scalar_prefetch=1,
            in_specs=[VSPEC] * 2 + [ANY] * 6,
            out_specs=[ANY] * 5,
            scratch_shapes=[
                pltpu.VMEM((SHARDS, ROWS, 128), F32),
                pltpu.VMEM((SPLIT, QS, HEAD, 128), F32),
                pltpu.VMEM((SPLIT, QS, ROWS, 128), F32),
                pltpu.VMEM((4, 8, 128), F32),
                pltpu.SemaphoreType.DMA((SPLIT, 2)),
                pltpu.SemaphoreType.DMA((SPLIT + 1,)),
            ],
        ),
        out_shape=[pltpu.HBM((QS, ROWS, 128), F32)] * 4 + [pltpu.HBM((SHARDS, ROWS, 128), F32)],
        input_output_aliases={4: 4},
        compiler_params=SMALL,
        name="make_update",
    )(me, *put([mv, own], pltpu.VMEM), *put([squares, grads, *ws], pltpu.HBM))


def add_body(x, out):
    out[...] = jnp.sum(x[:, HEAD:ROWS, :], axis=0)


def add_sums(x):
    return pl.pallas_call(
        add_body,
        in_specs=[VSPEC],
        out_specs=VSPEC,
        out_shape=jax.ShapeDtypeStruct((8, 128), F32),
        compiler_params=SMALL,
        name="add_sums",
    )(*put([x], pltpu.VMEM))


def moments_of(n, g, first, second):
    def step(at, grad):
        first[at] = beta_one * first[at] + (1.0 - beta_one) * grad
        second[at] = beta_two * second[at] + (1.0 - beta_two) * grad * grad

    every = slice(None)
    if n < 2:
        for c in range(0, SHARDS, 2):
            cols = slice(c * 64, c * 64 + 128)
            for pair in range(2 - n):
                rows = slice(32, 72) if n else slice(16 * pair, 16 * pair + 16)
                x = swap_halves(g[c, rows, :], g[c + 1, rows, :])
                for a in range(2):
                    step((2 * pair + a, every, cols), x[a])
        return
    lane = lanes((16, 128))
    for c in range(0, SHARDS, 4):
        before = rest = None
        for b in range(5):
            block = roll(g[c + b, 72:88, :], 32 * b) if b < 4 else None
            here = block
            if b > 0:
                here = rest if block is None else jnp.where(lane < 32 * b, rest, block)
                here = jnp.where(lane < 32 * (b - 1), before, here)
            at = c // 4 * 640 + b * 128
            step((0, every, slice(at, at + 128)), here)
            if b < 4:
                before = block
                tile = g[c + b, HEAD:ROWS, :]
                rest = jnp.concatenate([roll(tile, 32 * b), roll(tile, 32 * b - 32)], axis=0)


def moments_body(*refs):
    g, hbm, new, buf, sems, out_sems = refs[0], refs[1:7], refs[7:13], refs[13:19], refs[19], refs[20]
    loads = copies(list(zip(hbm, buf, strict=True)), sems)
    stores = copies(list(zip(buf, new, strict=True)), out_sems)
    order = (1, 0, 2)
    for n in order:
        start((loads[n], loads[n + 3]))
    for n in order:
        wait((loads[n], loads[n + 3]))
        moments_of(n, g, buf[n], buf[n + 3])
        start((stores[n], stores[n + 3]))
    wait(stores)


def new_moments(g, *moments):
    return pl.pallas_call(
        moments_body,
        in_specs=[VSPEC] + [ANY] * 6,
        out_specs=[ANY] * 6,
        out_shape=[pltpu.HBM(x.shape, F32) for x in moments],
        scratch_shapes=[pltpu.VMEM(x.shape, F32) for x in moments]
        + [pltpu.SemaphoreType.DMA((6,)), pltpu.SemaphoreType.DMA((6,))],
        compiler_params=SMALL,
        name="new_moments",
    )(*put([g], pltpu.VMEM), *put(moments, pltpu.HBM))


def k3b_body(me, s0, s1, s2, s3, u0, u1, u2, u3, attn, ffin, ffout, attn2, ffin2, ffout2, trust_out, turned):
    total = (s0[...] + s2[...]) + (s1[...] + s3[...])
    lane = lanes((8, 128))
    update_sq = jnp.sum(jnp.where((lane >= 64) & (lane < 96), total, 0.0), axis=1, keepdims=True)
    weight_sq = jnp.sum(jnp.where(lane >= 96, total, 0.0), axis=1, keepdims=True)
    trust = jnp.sqrt(weight_sq) / (jnp.sqrt(update_sq) + epsilon)
    for n in range(7):
        trust_out[n] = trust[n, 0]
    scale = learn_rate * trust
    here = pl.ds(pl.multiple_of(pl.program_id(0) * 4, 4), 4)
    for d, u in enumerate((u0, u1.at[here], u2.at[here], u3.at[here])):
        source = lax.rem(me[0] + d, SPLIT)
        for q in range(4):
            place = q * SPLIT + source
            at = pl.multiple_of(place * 16, 16)
            for pair in range(2):
                turned[pl.ds(pair * 256 + at, 16), :] = u[q, 16 * pair : 16 * pair + 16, :]
            turned[pl.ds(512 + pl.multiple_of(place * 40, 8), 40), :] = u[q, 32:72, :]
            turned[pl.ds(1152 + at, 16), :] = u[q, 72:88, :]
            tile = u[q, 88:96, :]
            turned[pl.ds(1408 + at, 8), :] = tile
            turned[pl.ds(1416 + at, 8), :] = roll(tile, -32)
    for pair in range(2):
        back = turned[pair * 256 : pair * 256 + 256, :].T
        for a in range(2):
            n = 2 * pair + a
            attn2[n] = attn[n] - scale[n : n + 1] * back[64 * a : 64 * a + 64]
    back = turned[512:1152, :].T
    for a in range(2):
        ffin2[a] = ffin[a] - scale[4 + a : 5 + a] * back[64 * a : 64 * a + 64]
    ffout2[0, 0:128, :] = ffout[0, 0:128, :] - scale[6:7] * turned[1152:1408, :].T
    ffout2[0, 128:160, :] = ffout[0, 128:160, :] - scale[6:7] * turned[1408:1664, :].T[0:32]


def new_weights(me, sums, us, attn, ffin, ffout):
    return pl.pallas_call(
        k3b_body,
        grid_spec=pltpu.PrefetchScalarGridSpec(
            num_scalar_prefetch=1,
            grid=(2,),
            in_specs=[VSPEC] * 4 + [pl.BlockSpec((4, ROWS, 128), lambda i, *_: (i, 0, 0))] + [VSPEC] * 3 + weight_specs(),
            out_specs=weight_specs() + [pl.BlockSpec(memory_space=pltpu.SMEM)],
            scratch_shapes=[pltpu.VMEM((1664, 128), F32)],
        ),
        out_shape=[pltpu.HBM(x.shape, F32) for x in (attn, ffin, ffout)] + [jax.ShapeDtypeStruct((7,), F32)],
        compiler_params=SMALL,
        name="new_weights",
    )(
        me,
        *put(sums, pltpu.VMEM),
        *put(us[:1], pltpu.HBM),
        *put(us[1:], pltpu.VMEM),
        *put([attn, ffin, ffout], pltpu.HBM),
    )


ORDER = (1, 3, 2)


def along(x, shift):
    shift %= SPLIT
    if shift == 0:
        return x
    return lax.ppermute(x, "tensor", [(i, (i + shift) % SPLIT) for i in range(SPLIT)])


def shards(aw, fw, ow, ag, fg, og, am, fm, om, av, fv, ov):
    t = lax.axis_index("tensor").astype(jnp.int32)
    me = t.reshape(1)
    mv, *g = pack_first(me, (am, fm, om, av, fv, ov), (ag, fg, og), ow)
    mv_here = lax.all_to_all(mv, "shard", split_axis=0, concat_axis=0, tiled=True)
    for d in ORDER:
        g[d] = along(g[d], d)
    w = list(pack_weights(me, (aw, fw, ow)))
    for d in ORDER:
        w[d] = along(w[d], d)
    grads, squares = gather_grads(me, g, (aw, fw, ow))
    *us, grads = make_update(me, mv_here, g[0], squares, grads, w)
    us = list(us)
    for d in (2, 1, 3):
        us[d] = along(us[d], -d)
    grads = lax.all_to_all(grads, "shard", split_axis=0, concat_axis=0, tiled=True)
    sums = add_sums(grads)
    sums = [along(sums, d) for d in range(SPLIT)]
    moments = new_moments(grads, am, fm, om, av, fv, ov)
    aw2, fw2, ow2, trust = new_weights(me, sums, us, aw, fw, ow)
    return (aw2, fw2, ow2, *moments, trust)


def solution(mesh):
    home = P(None, "shard", "tensor")
    flat = P(None, ("shard", "tensor"), None)
    in_specs = (home,) * 6 + (flat,) * 6
    out_specs = (home,) * 3 + (flat,) * 6 + (P(),)
    return jax.shard_map(shards, mesh=mesh, in_specs=in_specs, out_specs=out_specs, check_vma=False)
```

```python
import jax
import jax.numpy as jnp
from jax import lax
from jax.experimental import pallas as pl
from jax.experimental.pallas import tpu as pltpu
from jax.sharding import PartitionSpec as P

beta_one = 0.9
beta_two = 0.999
step_number = 10.0
correct_one = 1.0 - beta_one**step_number
correct_two = 1.0 - beta_two**step_number
learn_rate = 0.02
decay_rate = 0.1
epsilon = 1e-06

F32 = jnp.float32
SHARDS = 32
SPLIT = 4
QS = SHARDS // SPLIT
HEAD = 88
ROWS = 96


ANY = pl.BlockSpec(memory_space=pl.ANY)
VSPEC = pl.BlockSpec(memory_space=pltpu.VMEM)
SMALL = pltpu.CompilerParams(vmem_limit_bytes=24 * 2**20)

def put(xs, space):
    return [pltpu.with_memory_space_constraint(x, space) for x in xs]


def copies(pairs, sems):
    return [pltpu.make_async_copy(a, b, sems.at[n]) for n, (a, b) in enumerate(pairs)]


def start(cs):
    for c in cs:
        c.start()


def wait(cs):
    for c in cs:
        c.wait()


def lanes(shape):
    return lax.broadcasted_iota(jnp.int32, shape, len(shape) - 1)


def roll(x, shift):
    shift %= 128
    return pltpu.roll(x, shift, x.ndim - 1) if shift else x


def swap_halves(x0, x1):
    low = lanes(x0.shape) < 64
    turned = roll(jnp.where(low, x1, x0), 64)
    return jnp.where(low, x0, turned), jnp.where(low, turned, x1)


def pack_moments(n, first, second, out):
    if n < 2:
        for c in range(0, SHARDS, 2):
            cols = slice(c * 64, c * 64 + 128)
            for base, moment in ((0, first), (HEAD, second)):
                for pair in range(2 - n):
                    rows = slice(base + 32, base + 72) if n else slice(base + 16 * pair, base + 16 * pair + 16)
                    x = swap_halves(moment[2 * pair, :, cols], moment[2 * pair + 1, :, cols])
                    for a in range(2):
                        out[c + a, rows, :] = x[a]
        return
    lane = lanes((16, 128))
    low = lanes((8, 128))
    for c in range(SHARDS):
        e, at = c % 4, c // 4 * 640 + c % 4 * 128
        last = []
        for base, moment in ((0, first), (HEAD, second)):
            x = moment[0, :, at : at + 128]
            y = moment[0, :, at + 128 : at + 256]
            main = jnp.where(lane < 128 - 32 * e, roll(x, -32 * e), roll(y, -32 * e))
            out[c, base + 72 : base + 88, :] = main
            last.append(y)
        tile = jnp.where(low < 32, roll(last[0][0:8], -32 * e), roll(last[0][8:16], 32 - 32 * e))
        other = jnp.where(low < 96, roll(last[1][0:8], 64 - 32 * e), roll(last[1][8:16], 96 - 32 * e))
        out[c, 2 * HEAD :, :] = jnp.where(low < 64, tile, other)


PACKED = (((0, 32), (88, 120)), ((32, 72), (120, 160)), ((72, 88), (160, 184)))


def square_sum(x):
    return jnp.sum((x * x).reshape(-1, 8, 128), axis=0)


def turn(attn, ffin, ffout, last, turned):
    for pair in range(2):
        both = jnp.concatenate([attn[2 * pair], attn[2 * pair + 1]], axis=0)
        turned[pair * 512 : pair * 512 + 512, :] = both.T
    turned[1024:2304, :] = jnp.concatenate([ffin[0], ffin[1]], axis=0).T
    turned[2304:2816, :] = ffout[0, 0:128, :].T
    if last is not None:
        turned[2816:3328, :] = last.T


def turned_rows(place):
    small = pl.multiple_of(place * 16, 16)
    large = pl.multiple_of(place * 40, 8)
    return (
        ((0, 16), small),
        ((16, 32), 512 + small),
        ((32, 72), 1024 + large),
        ((72, 88), 2304 + small),
    )


def deal(me, turned, out, whole):
    lane = lanes((8, 128))
    for d in range(SPLIT):
        target = lax.rem(me + d, SPLIT)
        for q in range(QS):
            place = q * SPLIT + target
            for (lo, hi), at in turned_rows(place):
                out[d, q, lo:hi, :] = turned[pl.ds(at, hi - lo), :]
            if whole:
                at = pl.multiple_of(2816 + place * 16, 8)
                v0, v1 = turned[pl.ds(at, 8), :], turned[pl.ds(at + 8, 8), :]
                high = jnp.where(lane < 96, roll(v0, 32), roll(v1, 64))
                low = jnp.where(lane < 32, v0, roll(v1, 32))
                out[d, q, HEAD:ROWS, :] = jnp.where(lane < 64, low, high)


def pack_first_body(*refs):
    me, hbm, grads, weight, out, pieces = refs[0], refs[1:7], refs[7:10], refs[10], refs[11], refs[12:16]
    buf, packed, gbuf, wbuf, turned, dealt = refs[16:22], refs[22], refs[23:26], refs[26], refs[27], refs[28]
    sems, out_sems, grad_sems, piece_sems = refs[29:]
    loads = copies(list(zip(hbm, buf, strict=True)), sems)
    pairs = list(zip(grads, gbuf, strict=True)) + [(weight.at[0, 128:160], wbuf)]
    grad_loads = copies(pairs, grad_sems)
    stores = [
        copies([(packed.at[:, lo:hi], out.at[:, lo:hi]) for lo, hi in rows], out_sems.at[n])
        for n, rows in enumerate(PACKED)
    ]
    piece_stores = copies([(dealt.at[d], pieces[d]) for d in range(SPLIT)], piece_sems)
    order = (1, 0, 2)
    for n in order:
        start((loads[n], loads[n + 3]))
    start(grad_loads)
    for n in order:
        wait((loads[n], loads[n + 3]))
        pack_moments(n, buf[n], buf[n + 3], packed)
        start(stores[n])
    wait(grad_loads)
    last = jnp.concatenate([gbuf[2][0, 128:160, :], wbuf[...], jnp.zeros((64, 512), F32)], axis=0)
    turn(*gbuf, last, turned)
    deal(me[0], turned, dealt, True)
    start(piece_stores)
    for n in order:
        wait(stores[n])
    wait(piece_stores)


def pack_first(me, moments, grads, weight):
    shape = (SHARDS, 2 * HEAD + 8, 128)
    dma = pltpu.SemaphoreType.DMA
    return pl.pallas_call(
        pack_first_body,
        grid_spec=pltpu.PrefetchScalarGridSpec(
            num_scalar_prefetch=1,
            in_specs=[ANY] * 10,
            out_specs=[ANY, VSPEC] + [ANY] * 3,
            scratch_shapes=[pltpu.VMEM(x.shape, F32) for x in moments]
            + [pltpu.VMEM(shape, F32)]
            + [pltpu.VMEM(x.shape, F32) for x in grads]
            + [
                pltpu.VMEM((32, 512), F32),
                pltpu.VMEM((3328, 128), F32),
                pltpu.VMEM((SPLIT, QS, ROWS, 128), F32),
                dma((6,)),
                dma((3, 2)),
                dma((4,)),
                dma((SPLIT,)),
            ],
        ),
        out_shape=[jax.ShapeDtypeStruct(shape, F32), pltpu.VMEM((QS, ROWS, 128), F32)]
        + [jax.ShapeDtypeStruct((QS, ROWS, 128), F32)] * 3,
        name="pack_first",
    )(me, *moments, *grads, weight)


def pack_weights_body(*refs):
    me, weights, pieces, buf, turned, dealt, sems, piece_sems = refs[0], refs[1:4], refs[4:8], refs[8:11], *refs[11:]
    loads = copies(list(zip(weights, buf, strict=True)), sems)
    piece_stores = copies([(dealt.at[d], pieces[d]) for d in range(SPLIT)], piece_sems)
    start(loads)
    wait(loads)
    turn(*buf, None, turned)
    deal(me[0], turned, dealt, False)
    start(piece_stores)
    wait(piece_stores)


def pack_weights(me, weights):
    return pl.pallas_call(
        pack_weights_body,
        grid_spec=pltpu.PrefetchScalarGridSpec(
            num_scalar_prefetch=1,
            in_specs=[ANY] * 3,
            out_specs=[ANY] * 4,
            scratch_shapes=[pltpu.VMEM(x.shape, F32) for x in weights]
            + [
                pltpu.VMEM((2816, 128), F32),
                pltpu.VMEM((SPLIT, QS, HEAD, 128), F32),
                pltpu.SemaphoreType.DMA((3,)),
                pltpu.SemaphoreType.DMA((SPLIT,)),
            ],
        ),
        out_shape=[jax.ShapeDtypeStruct((QS, HEAD, 128), F32)] * 4,
        name="pack_weights",
    )(me, *weights)


def gather_body(*refs):
    me, g_own, g_hbm, weights, out, squares_hbm = refs[0], refs[1], refs[2:5], refs[5:8], refs[8], refs[9]
    buf, gbuf, squares, sems, grad_sems, out_sems = refs[10:13], *refs[13:]
    moves = []
    for d, g in enumerate((g_own, *(gbuf.at[n] for n in range(3)))):
        block = pl.ds(pl.multiple_of(lax.rem(me[0] + SPLIT - d, SPLIT) * QS, QS), QS)
        moves.append(pltpu.make_async_copy(g, out.at[block], out_sems.at[d]))
    loads = copies(list(zip(weights, buf, strict=True)), sems)
    grad_loads = copies([(g, gbuf.at[n]) for n, g in enumerate(g_hbm)], grad_sems)
    start(grad_loads)
    start(loads)
    moves[0].start()
    wait(grad_loads)
    start(moves[1:])
    wait(loads)
    attn, ffin, ffout = buf

    def total(x):
        return sum(square_sum(x[:, n : n + 128]) for n in range(0, x.shape[1], 128))

    low = lanes((8, 128)) < 64
    for n, (x, y) in enumerate(((attn[0], attn[1]), (attn[2], attn[3]), (ffin[0], ffin[1]))):
        x, y = total(x), total(y)
        squares[n] = jnp.where(low, x + roll(x, 64), y + roll(y, 64))
    squares[3] = total(ffout[0])
    done = pltpu.make_async_copy(squares, squares_hbm, out_sems.at[SPLIT])
    done.start()
    wait(moves)
    done.wait()


def gather_grads(me, gs, weights):
    return pl.pallas_call(
        gather_body,
        grid_spec=pltpu.PrefetchScalarGridSpec(
            num_scalar_prefetch=1,
            in_specs=[VSPEC] + [ANY] * 6,
            out_specs=[ANY] * 2,
            scratch_shapes=[pltpu.VMEM(x.shape, F32) for x in weights]
            + [
                pltpu.VMEM((3, QS, ROWS, 128), F32),
                pltpu.VMEM((4, 8, 128), F32),
                pltpu.SemaphoreType.DMA((3,)),
                pltpu.SemaphoreType.DMA((3,)),
                pltpu.SemaphoreType.DMA((SPLIT + 1,)),
            ],
        ),
        out_shape=[pltpu.HBM((SHARDS, ROWS, 128), F32), pltpu.HBM((4, 8, 128), F32)],
        name="gather_grads",
    )(me, *put(gs[:1], pltpu.VMEM), *put([*gs[1:], *weights], pltpu.HBM))


def weight_specs():
    return [
        pl.BlockSpec((4, 64, 256), lambda i, *_: (0, 0, i)),
        pl.BlockSpec((2, 64, 640), lambda i, *_: (0, 0, i)),
        pl.BlockSpec((1, 160, 256), lambda i, *_: (0, 0, i)),
    ]


GROUPS = ((0, 16), (16, 32), (32, 72), (72, 88))
FIRST_SCALE = 1.0 / correct_one
SECOND_SCALE = 1.0 / correct_two


def ratio_of(grad, first, second):
    first = beta_one * first + (1.0 - beta_one) * grad
    second = beta_two * second + (1.0 - beta_two) * grad * grad
    return first * FIRST_SCALE / (jnp.sqrt(second * SECOND_SCALE) + epsilon)


def update_body(*refs):
    me, mv, g_own, squares_hbm, g_hbm, w_hbm, u_hbm, out = *refs[0:5], refs[5:9], refs[9:13], refs[13]
    g, w, u, squares, sems, out_sems = refs[14:]
    places = [pl.multiple_of(lax.rem(me[0] + SPLIT - d, SPLIT) * QS, QS) for d in range(SPLIT)]
    blocks = [pl.ds(at, QS) for at in places]
    grad_loads = [pltpu.make_async_copy(g_hbm.at[b], g.at[b], sems.at[d, 0]) for d, b in enumerate(blocks) if d]
    loads = [pltpu.make_async_copy(w_hbm[d], w.at[d], sems.at[d, 1]) for d in range(SPLIT)]
    stores = copies([(u.at[d], u_hbm[d]) for d in range(SPLIT)], out_sems)
    last = pltpu.make_async_copy(g.at[:, HEAD:ROWS], out.at[:, HEAD:ROWS], out_sems.at[SPLIT])
    square_load = pltpu.make_async_copy(squares_hbm, squares, sems.at[0, 0])
    loads[0].start()
    for d in range(1, SPLIT):
        grad_loads[d - 1].start()
        loads[d].start()
    square_load.start()
    low = lanes((8, 128)) < 64

    def ratio_rows(n, q, at, grad):
        if n < 4:
            lo, hi = GROUPS[n]
            return ratio_of(grad, mv[at + q, lo:hi, :], mv[at + q, HEAD + lo : HEAD + hi, :])
        tile = mv[at + q, 2 * HEAD :, :]
        return jnp.where(low, ratio_of(grad, tile, jnp.where(low, roll(tile, 64), 1.0)), 0.0)

    def own_ratio(q, carry):
        for n, (lo, hi) in enumerate((*GROUPS, (HEAD, ROWS))):
            grad = g_own[q, lo:hi, :]
            if n == 4:
                g[places[0] + q, lo:hi, :] = grad
            u[0, q, lo:hi, :] = ratio_rows(n, q, places[0], grad)
        return carry

    lax.fori_loop(0, QS, own_ratio, 0, unroll=8)
    totals = (jnp.zeros((8, 128), F32),) * 4
    for d in range(SPLIT):
        if d:
            grad_loads[d - 1].wait()
        loads[d].wait()

        def chunk(q, totals, d=d):
            totals = list(totals)
            at = places[d]
            for n, (lo, hi) in enumerate((*GROUPS, (HEAD, ROWS))):
                if d or n == 4:
                    grad = g[at + q, lo:hi, :]
                ratio = ratio_rows(n, q, at, grad) if d else u[0, q, lo:hi, :]
                weight = w[d, q, lo:hi, :] if n < 4 else jnp.where(low, roll(grad, 64), 0.0)
                update = ratio + decay_rate * weight
                u[d, q, lo:hi, :] = update
                totals[min(n, 3)] += square_sum(update)
            return tuple(totals)

        totals = lax.fori_loop(0, QS, chunk, totals, unroll=8)
        stores[d].start()
    square_load.wait()
    totals = [*totals, *(squares[n] for n in range(4))]
    total = jnp.concatenate([jnp.sum(x, axis=0, keepdims=True) for x in totals], axis=0)
    fold = total + roll(total, 96)
    lane = lanes((1, 128))
    rows = []
    for matrix in range(7):
        parts = []
        for kind in range(2):
            group = kind * 4 + (3 if matrix == 6 else matrix // 2)
            row = fold[group : group + 1]
            if matrix == 6:
                row = row + roll(row, 64)
            elif matrix % 2:
                row = roll(row, 64)
            parts.append(row)
        rows.append(jnp.where(lane < 96, roll(parts[0], 64), roll(parts[1], 96)))
    rows.append(jnp.zeros((1, 128), F32))
    sums = jnp.concatenate(rows, axis=0)
    for n in range(SHARDS):
        g[n, HEAD:ROWS, :] = jnp.where(low, g[n, HEAD:ROWS, :], sums)
    last.start()
    wait(stores)
    last.wait()


def make_update(me, mv, own, squares, grads, ws):
    return pl.pallas_call(
        update_body,
        grid_spec=pltpu.PrefetchScalarGridSpec(
            num_scalar_prefetch=1,
            in_specs=[VSPEC] * 2 + [ANY] * 6,
            out_specs=[ANY] * 5,
            scratch_shapes=[
                pltpu.VMEM((SHARDS, ROWS, 128), F32),
                pltpu.VMEM((SPLIT, QS, HEAD, 128), F32),
                pltpu.VMEM((SPLIT, QS, ROWS, 128), F32),
                pltpu.VMEM((4, 8, 128), F32),
                pltpu.SemaphoreType.DMA((SPLIT, 2)),
                pltpu.SemaphoreType.DMA((SPLIT + 1,)),
            ],
        ),
        out_shape=[pltpu.HBM((QS, ROWS, 128), F32)] * 4 + [pltpu.HBM((SHARDS, ROWS, 128), F32)],
        input_output_aliases={4: 4},
        compiler_params=SMALL,
        name="make_update",
    )(me, *put([mv, own], pltpu.VMEM), *put([squares, grads, *ws], pltpu.HBM))


def add_body(x, out):
    out[...] = jnp.sum(x[:, HEAD:ROWS, :], axis=0)


def add_sums(x):
    return pl.pallas_call(
        add_body,
        in_specs=[VSPEC],
        out_specs=VSPEC,
        out_shape=jax.ShapeDtypeStruct((8, 128), F32),
        compiler_params=SMALL,
        name="add_sums",
    )(*put([x], pltpu.VMEM))


def moments_of(n, g, first, second):
    def step(at, grad):
        first[at] = beta_one * first[at] + (1.0 - beta_one) * grad
        second[at] = beta_two * second[at] + (1.0 - beta_two) * grad * grad

    every = slice(None)
    if n < 2:
        for c in range(0, SHARDS, 2):
            cols = slice(c * 64, c * 64 + 128)
            for pair in range(2 - n):
                rows = slice(32, 72) if n else slice(16 * pair, 16 * pair + 16)
                x = swap_halves(g[c, rows, :], g[c + 1, rows, :])
                for a in range(2):
                    step((2 * pair + a, every, cols), x[a])
        return
    lane = lanes((16, 128))
    for c in range(0, SHARDS, 4):
        before = rest = None
        for b in range(5):
            block = roll(g[c + b, 72:88, :], 32 * b) if b < 4 else None
            here = block
            if b > 0:
                here = rest if block is None else jnp.where(lane < 32 * b, rest, block)
                here = jnp.where(lane < 32 * (b - 1), before, here)
            at = c // 4 * 640 + b * 128
            step((0, every, slice(at, at + 128)), here)
            if b < 4:
                before = block
                tile = g[c + b, HEAD:ROWS, :]
                rest = jnp.concatenate([roll(tile, 32 * b), roll(tile, 32 * b - 32)], axis=0)


def moments_body(*refs):
    g, hbm, new, buf, sems, out_sems = refs[0], refs[1:7], refs[7:13], refs[13:19], refs[19], refs[20]
    loads = copies(list(zip(hbm, buf, strict=True)), sems)
    stores = copies(list(zip(buf, new, strict=True)), out_sems)
    order = (1, 0, 2)
    for n in order:
        start((loads[n], loads[n + 3]))
    for n in order:
        wait((loads[n], loads[n + 3]))
        moments_of(n, g, buf[n], buf[n + 3])
        start((stores[n], stores[n + 3]))
    wait(stores)


def new_moments(g, *moments):
    return pl.pallas_call(
        moments_body,
        in_specs=[VSPEC] + [ANY] * 6,
        out_specs=[ANY] * 6,
        out_shape=[pltpu.HBM(x.shape, F32) for x in moments],
        scratch_shapes=[pltpu.VMEM(x.shape, F32) for x in moments]
        + [pltpu.SemaphoreType.DMA((6,)), pltpu.SemaphoreType.DMA((6,))],
        compiler_params=SMALL,
        name="new_moments",
    )(*put([g], pltpu.VMEM), *put(moments, pltpu.HBM))


def k3b_body(me, s0, s1, s2, s3, u0, u1, u2, u3, attn, ffin, ffout, attn2, ffin2, ffout2, trust_out, turned):
    total = (s0[...] + s2[...]) + (s1[...] + s3[...])
    lane = lanes((8, 128))
    update_sq = jnp.sum(jnp.where((lane >= 64) & (lane < 96), total, 0.0), axis=1, keepdims=True)
    weight_sq = jnp.sum(jnp.where(lane >= 96, total, 0.0), axis=1, keepdims=True)
    trust = jnp.sqrt(weight_sq) / (jnp.sqrt(update_sq) + epsilon)
    for n in range(7):
        trust_out[n] = trust[n, 0]
    scale = learn_rate * trust
    here = pl.ds(pl.multiple_of(pl.program_id(0) * 4, 4), 4)
    for d, u in enumerate((u0, u1.at[here], u2.at[here], u3.at[here])):
        source = lax.rem(me[0] + d, SPLIT)
        for q in range(4):
            place = q * SPLIT + source
            at = pl.multiple_of(place * 16, 16)
            for pair in range(2):
                turned[pl.ds(pair * 256 + at, 16), :] = u[q, 16 * pair : 16 * pair + 16, :]
            turned[pl.ds(512 + pl.multiple_of(place * 40, 8), 40), :] = u[q, 32:72, :]
            turned[pl.ds(1152 + at, 16), :] = u[q, 72:88, :]
            tile = u[q, 88:96, :]
            turned[pl.ds(1408 + at, 8), :] = tile
            turned[pl.ds(1416 + at, 8), :] = roll(tile, -32)
    for pair in range(2):
        back = turned[pair * 256 : pair * 256 + 256, :].T
        for a in range(2):
            n = 2 * pair + a
            attn2[n] = attn[n] - scale[n : n + 1] * back[64 * a : 64 * a + 64]
    back = turned[512:1152, :].T
    for a in range(2):
        ffin2[a] = ffin[a] - scale[4 + a : 5 + a] * back[64 * a : 64 * a + 64]
    ffout2[0, 0:128, :] = ffout[0, 0:128, :] - scale[6:7] * turned[1152:1408, :].T
    ffout2[0, 128:160, :] = ffout[0, 128:160, :] - scale[6:7] * turned[1408:1664, :].T[0:32]


def new_weights(me, sums, us, attn, ffin, ffout):
    return pl.pallas_call(
        k3b_body,
        grid_spec=pltpu.PrefetchScalarGridSpec(
            num_scalar_prefetch=1,
            grid=(2,),
            in_specs=[VSPEC] * 4 + [pl.BlockSpec((4, ROWS, 128), lambda i, *_: (i, 0, 0))] + [VSPEC] * 3 + weight_specs(),
            out_specs=weight_specs() + [pl.BlockSpec(memory_space=pltpu.SMEM)],
            scratch_shapes=[pltpu.VMEM((1664, 128), F32)],
        ),
        out_shape=[pltpu.HBM(x.shape, F32) for x in (attn, ffin, ffout)] + [jax.ShapeDtypeStruct((7,), F32)],
        compiler_params=SMALL,
        name="new_weights",
    )(
        me,
        *put(sums, pltpu.VMEM),
        *put(us[:1], pltpu.HBM),
        *put(us[1:], pltpu.VMEM),
        *put([attn, ffin, ffout], pltpu.HBM),
    )


ORDER = (1, 3, 2)


def along(x, shift):
    shift %= SPLIT
    if shift == 0:
        return x
    return lax.ppermute(x, "tensor", [(i, (i + shift) % SPLIT) for i in range(SPLIT)])


def shards(aw, fw, ow, ag, fg, og, am, fm, om, av, fv, ov):
    t = lax.axis_index("tensor").astype(jnp.int32)
    me = t.reshape(1)
    mv, *g = pack_first(me, (am, fm, om, av, fv, ov), (ag, fg, og), ow)
    mv_here = lax.all_to_all(mv, "shard", split_axis=0, concat_axis=0, tiled=True)
    for d in ORDER:
        g[d] = along(g[d], d)
    w = list(pack_weights(me, (aw, fw, ow)))
    for d in ORDER:
        w[d] = along(w[d], d)
    grads, squares = gather_grads(me, g, (aw, fw, ow))
    *us, grads = make_update(me, mv_here, g[0], squares, grads, w)
    us = list(us)
    for d in (2, 1, 3):
        us[d] = along(us[d], -d)
    grads = lax.all_to_all(grads, "shard", split_axis=0, concat_axis=0, tiled=True)
    sums = add_sums(grads)
    sums = [along(sums, d) for d in range(SPLIT)]
    moments = new_moments(grads, am, fm, om, av, fv, ov)
    aw2, fw2, ow2, trust = new_weights(me, sums, us, aw, fw, ow)
    return (aw2, fw2, ow2, *moments, trust)


def solution(mesh):
    home = P(None, "shard", "tensor")
    flat = P(None, ("shard", "tensor"), None)
    in_specs = (home,) * 6 + (flat,) * 6
    out_specs = (home,) * 3 + (flat,) * 6 + (P(),)
    return jax.shard_map(shards, mesh=mesh, in_specs=in_specs, out_specs=out_specs, check_vma=False)
```
